256 devices in a mesh: epoch: 32 (over x, z), param: 8 (over y, core).
Axes of the slice: x: 4, y: 4, z: 8, core: 2. Of those that a mesh axis runs over, the one named last changes fastest.
Arguments:
- initial_carry: float32 [48, 8192], P(None, 'param'), may hold values from -6 to 6
- forcing: bfloat16 [128, 48, 8192], P('epoch', None, 'param'), may hold values from -2.390625 to 2.390625
- transition: float32 [128, 6, 6, 8], P('epoch'), may hold values from -0.2 to 1.2
- partials: float32 [6, 4096], P(None, 'epoch'), may hold values from -40 to 40
- arc_of_row: int32 [4096], P('epoch'), may hold values from 0 to 7
- counts: int32 [128], P('epoch'), may hold values from 8 to 32
Outputs:
- packed: float32 [4096, 8192], P('epoch', 'param')
- r_rows: float32 [512, 8192], P(None, 'param')
The draws below stay inside these ranges and needn't reach their ends.
Inputs may be any that keep to these rules, and one draw needn't show every extreme that they name: Rows of block j at positions counts[j] and beyond carry no observation.
All inputs are finite; a program needn't handle non-finite values.
Results may differ from the reference program's by a relative error of at most 0.0003.
Values sent between devices are 32-bit elements; how exact they have to be, the bound alone decides.
No kernel may reach another device: no remote copies, remote signals or barrier semaphores. Data moves between devices by JAX's collectives and lax.ppermute only.
A program may use at most 64 MiB of HBM per device.

```python
import math
import jax
import jax.numpy as jnp
from jax import lax

PARAMS = 8192
PANEL = 256
STATE = 6
ARCS = 8
BLOCK_ROWS = 32
TIME_SPAN_COUNT = 128
ROWS = 4096
ARC_ROWS = 48


def draw_transition(key, part):
    partial_derivative_transfers = jax.random.split(key, 6)
    slow_share = 0.5
    slow_arcs = jax.random.uniform(partial_derivative_transfers[0], (ARCS,)) < slow_share
    strength = jax.random.uniform(partial_derivative_transfers[1], (ARCS,), minval=0.1, maxval=0.4)
    jitter = jax.random.uniform(partial_derivative_transfers[2], (TIME_SPAN_COUNT, ARCS), minval=0.5, maxval=1.5)
    slow_decay = jnp.exp(jnp.log(0.1) * strength[None, :] * jitter / TIME_SPAN_COUNT)
    fast_decay = jax.random.uniform(partial_derivative_transfers[3], (TIME_SPAN_COUNT, ARCS), minval=0.3, maxval=0.6)
    damping_multipliers = jnp.where(slow_arcs[None, :], slow_decay, fast_decay)
    pulse_first_offset = jax.random.randint(partial_derivative_transfers[4], (3,), 0, TIME_SPAN_COUNT)
    pulse_line_cluster = jnp.any(jnp.arange(TIME_SPAN_COUNT)[:, None] == pulse_first_offset[None, :], axis=1)
    damping_multipliers = damping_multipliers * jnp.where(pulse_line_cluster, 0.7, 1.0)[:, None]
    perturb = jnp.clip(jax.random.normal(partial_derivative_transfers[5], (TIME_SPAN_COUNT, STATE, STATE, ARCS)), -4.0, 4.0)
    identity_block = jnp.eye(STATE, dtype=jnp.float32)[None, :, :, None]
    return damping_multipliers[:, None, None, :] * (identity_block + 0.1 / jnp.sqrt(6.0) * perturb)


def draw_partials(key, part):
    partial_derivative_transfers = jax.random.split(key, 2)
    row_scale = jnp.exp(jax.random.uniform(partial_derivative_transfers[0], (1, ROWS), minval=0.0, maxval=jnp.log(10.0)))
    values = jnp.clip(jax.random.normal(partial_derivative_transfers[1], (STATE, ROWS)), -4.0, 4.0)
    return values * row_scale


def plant(drawn, stream_key, smallest, top_value):
    spot = [jax.random.randint(jax.random.fold_in(stream_key, axis), (), 0, length) for axis, length in enumerate(drawn.shape)]
    main_axis = drawn.shape.index(max(drawn.shape))
    neighbour = spot[:main_axis] + [(spot[main_axis] + 1) % drawn.shape[main_axis]] + spot[main_axis + 1:]
    return drawn.at[tuple(spot)].set(smallest).at[tuple(neighbour)].set(top_value)


def levels(key, dims, cuts, least, high):
    gain = 1.0
    for dim, shards_of in cuts:
        steps = jax.random.uniform(jax.random.fold_in(jax.random.fold_in(key, 6), dim), (shards_of,), jnp.float32, least / len(cuts), high / len(cuts))
        gain = gain * jnp.repeat(jnp.exp(steps), dims[dim] // shards_of).reshape((-1,) + (1,) * (len(dims) - 1 - dim))
    return gain


def centred(own_key, shape, width, reach, cuts=(), kind=jnp.bfloat16):
    drawn = jax.random.normal(own_key, shape, jnp.float32) * width
    if len(cuts) > 0:
        drawn = levels(own_key, shape, cuts, -0.22, 0.18) * drawn
    return jnp.clip(drawn, min=-reach, max=reach).astype(kind)


def setup_inputs(seed: int = 0) -> dict:
    key_list = jax.random.split(jax.random.key(seed), 7)
    initial_carry = centred(key_list[0], (ARC_ROWS, PARAMS), 1.0, 6.0, ((1, 8),), jnp.float32)
    forcing = centred(key_list[1], (TIME_SPAN_COUNT, ARC_ROWS, PARAMS), 0.3, 2.390625, ((0, 32), (2, 8)))
    transition = draw_transition(jax.random.fold_in(key_list[6], 71), 0)
    partials = draw_partials(jax.random.fold_in(key_list[6], 71), 0)
    arc_of_row = plant(jax.random.randint(key_list[4], (ROWS,), 0, ARCS), jax.random.fold_in(key_list[4], 1), 0, ARCS - 1).astype(jnp.int32)
    counts = plant(jax.random.randint(key_list[5], (TIME_SPAN_COUNT,), BLOCK_ROWS // 4, BLOCK_ROWS + 1), jax.random.fold_in(key_list[5], 1), BLOCK_ROWS // 4, BLOCK_ROWS).astype(jnp.int32)
    return {"initial_carry": initial_carry, "forcing": forcing, "transition": transition, "partials": partials, "arc_of_row": arc_of_row, "counts": counts}


def propagate(carry, transition_step, driving_increment):
    states = transition_step.shape[0]
    view = carry.reshape(states, transition_step.shape[2], carry.shape[1])
    moved = jnp.einsum('cda,dap->cap', transition_step, view, precision=lax.Precision.HIGHEST)
    return moved.reshape(carry.shape) + driving_increment.astype(jnp.float32)

def observe(carry, partial_rows, orbit_track_lines, observed):
    arc_total = carry.shape[0] // partial_rows.shape[0]
    length = partial_rows.shape[1]
    live_rows = (jnp.arange(length) < observed).astype(jnp.float32)
    chosen = (orbit_track_lines[:, None] == jnp.arange(arc_total)[None, :]).astype(jnp.float32)
    weights = partial_rows.T[:, :, None] * chosen[:, None, :] * live_rows[:, None, None]
    return jnp.dot(weights.reshape(length, carry.shape[0]), carry, precision=lax.Precision.HIGHEST)

def reduce_panel(matrix, panel_cols):
    products = jnp.dot(panel_cols.T, matrix, precision=lax.Precision.HIGHEST)
    gram_block = jnp.dot(panel_cols.T, panel_cols, precision=lax.Precision.HIGHEST)
    factor = jnp.linalg.cholesky(gram_block)
    row_block = jax.scipy.linalg.solve_triangular(factor, products, lower=True)
    orthonormal = jax.scipy.linalg.solve_triangular(factor, panel_cols.T, lower=True).T
    updated = matrix - jnp.dot(orthonormal, row_block, precision=lax.Precision.HIGHEST)
    return (updated, row_block, orthonormal)

def reference(initial_carry, forcing, transition, partials, arc_of_row, counts):
    block_partials = partials.reshape(STATE, TIME_SPAN_COUNT, BLOCK_ROWS).transpose(1, 0, 2)
    block_arcs = arc_of_row.reshape(TIME_SPAN_COUNT, BLOCK_ROWS)

    def advance(carry, inputs):
        driving_increment, transition_step, partial_rows, orbit_track_lines, observed = inputs
        carry = propagate(carry, transition_step, driving_increment)
        return (carry, observe(carry, partial_rows, orbit_track_lines, observed))
    closing_carry_state, stacked = lax.scan(advance, initial_carry, (forcing, transition, block_partials, block_arcs, counts))
    matrix = stacked.reshape(ROWS, PARAMS)
    row_parts = []
    basis_parts = []
    for number in range(2):
        panel_cols = matrix[:, number * PANEL:(number + 1) * PANEL]
        matrix, row_block, orthonormal = reduce_panel(matrix, panel_cols)
        row_parts.append(row_block)
        basis_parts.append(orthonormal)
    root_rows = math.sqrt(ROWS)
    head_cols = jnp.concatenate(basis_parts, 1) * root_rows
    packed = jnp.concatenate([head_cols, matrix[:, 2 * PANEL:]], 1)
    r_rows = jnp.concatenate(row_parts, 0) / root_rows
    return (packed, r_rows)
```

```python
import functools
import math

import jax
import jax.numpy as jnp
from jax import lax
from jax.experimental import pallas as pl
from jax.experimental.pallas import tpu as pltpu
from jax.sharding import Mesh
from jax.sharding import PartitionSpec as P

PANEL = 512
X, Z, Y, C = 4, 8, 4, 2
STATE, ARCS = 6, 8
S = STATE * ARCS
PACK = S + 8
HI = lax.Precision.HIGHEST
VMEM = pl.BlockSpec(memory_space=pltpu.VMEM)
SMEM = pl.BlockSpec(memory_space=pltpu.SMEM)


def call(kernel, out, n, cost, smem=()):
    flops, size = cost
    return pl.pallas_call(
        kernel,
        out_shape=out,
        in_specs=[SMEM if i in smem else VMEM for i in range(n)],
        out_specs=VMEM if not isinstance(out, (tuple, list)) else [VMEM] * len(out),
        cost_estimate=pl.CostEstimate(flops=flops, bytes_accessed=size, transcendentals=0),
    )


def dot(a, b, ca=1, cb=0):
    return lax.dot_general(a, b, (((ca,), (cb,)), ((), ())), precision=HI, preferred_element_type=jnp.float32)


def same_arc(rows, cols):
    i = lax.broadcasted_iota(jnp.int32, (rows, cols), 0)
    j = lax.broadcasted_iota(jnp.int32, (rows, cols), 1)
    return lax.rem(i, ARCS) == lax.rem(j, ARCS)


def gatherer():
    i = lax.broadcasted_iota(jnp.int32, (8, S), 0)
    j = lax.broadcasted_iota(jnp.int32, (8, S), 1)
    return (i == lax.div(j, ARCS)).astype(jnp.float32)


def opened(packed):
    rows = [jnp.broadcast_to(packed[d : d + 1, :], (ARCS, S)) for d in range(STATE)]
    return jnp.where(same_arc(S, S), jnp.concatenate(rows, 0), 0.0)


def offsets_kernel(d_ref, f_ref, o_ref):
    carry = f_ref[0].astype(jnp.float32)
    whole = d_ref[0]
    for j in range(1, d_ref.shape[0]):
        carry = dot(d_ref[j], carry) + f_ref[j].astype(jnp.float32)
        whole = dot(d_ref[j], whole)
    packed = dot(gatherer(), whole, 1, 1)
    for z in range(Z):
        o_ref[z, :S, :] = carry[:, z * 128 : (z + 1) * 128]
        o_ref[z, S:, :] = jnp.zeros((8, 128), jnp.float32)
        o_ref[z, S:, :S] = packed


def totals_kernel(r_ref, o_ref):
    total = r_ref[0, :S, :]
    whole = opened(r_ref[0, S:, :S])
    for z in range(1, Z):
        step = opened(r_ref[z, S:, :S])
        total = dot(step, total, 0, 0) + r_ref[z, :S, :]
        whole = dot(whole, step)
    o_ref[:S, :] = total
    o_ref[S:, :] = jnp.zeros((8, 128), jnp.float32)
    o_ref[S:, :S] = dot(gatherer(), whole)


def incoming_kernel(x_ref, t_ref, r_ref, i_ref, o_ref):
    here = x_ref[0]
    carry = i_ref[...]
    for x in range(X - 1):
        after = dot(opened(t_ref[x, S:, :S]), carry, 0, 0) + t_ref[x, :S, :]
        carry = jnp.where(x < here, after, carry)
    for z in range(Z):
        o_ref[z] = carry
        if z < Z - 1:
            carry = dot(opened(r_ref[z, S:, :S]), carry, 0, 0) + r_ref[z, :S, :]


def design_kernel(n_ref, i_ref, d_ref, f_ref, p_ref, a_ref, o_ref):
    blocks = d_ref.shape[0]
    rows = p_ref.shape[1]
    length = rows // blocks
    lane = lax.broadcasted_iota(jnp.int32, (ARCS, rows), 1)
    arc = lax.broadcasted_iota(jnp.int32, (ARCS, rows), 0)
    chosen = arc == a_ref[...]
    weights = []
    for j in range(blocks):
        live = (lane >= j * length) & (lane < j * length + jnp.minimum(n_ref[j], length)) & chosen
        for c in range(STATE):
            weights.append(jnp.where(live, p_ref[c : c + 1, :], 0.0))
    weights = jnp.concatenate(weights, 0)
    carry = jnp.concatenate([i_ref[z] for z in range(Z)], 1)
    carries = []
    for j in range(blocks):
        carry = dot(d_ref[j], carry) + f_ref[j].astype(jnp.float32)
        carries.append(carry)
    o_ref[...] = dot(weights, jnp.concatenate(carries, 0), 0, 0)


def factor_kernel(g_ref, x_ref, z_ref):
    n = g_ref.shape[0]
    z_ref[...] = g_ref[...]
    sub = lax.broadcasted_iota(jnp.int32, (8, 128), 0)
    lane = lax.broadcasted_iota(jnp.int32, (8, 128), 1)
    row_n = lax.broadcasted_iota(jnp.int32, (n, 128), 0)
    col_n = lax.broadcasted_iota(jnp.int32, (n, n), 1)
    row_nn = lax.broadcasted_iota(jnp.int32, (n, n), 0)
    col_b = lax.broadcasted_iota(jnp.int32, (128, n), 1)
    i128 = lax.broadcasted_iota(jnp.int32, (128, 128), 0)
    j128 = lax.broadcasted_iota(jnp.int32, (128, 128), 1)

    def block(k, _):
        at = pl.multiple_of(k * 128, 128)
        part = [z_ref[pl.ds(at + 8 * g, 8), pl.ds(at, 128)] for g in range(16)]
        for q in range(128):
            gq, sq = q // 8, q % 8
            row = part[gq][sq : sq + 1, :]
            inverse = 1.0 / row[:, q : q + 1]
            row = jnp.where(lane[:1] == q, inverse, row * inverse)
            row = jnp.broadcast_to(row, (8, 128))
            for g in range(gq, 16):
                column = jnp.broadcast_to(part[g][:, q : q + 1], (8, 128))
                if g == gq:
                    if sq == 7:
                        continue
                    column = jnp.where(sub > sq, column, 0.0)
                    kept = jnp.where((lane == q) & (sub > sq), 0.0, part[g])
                else:
                    kept = jnp.where(lane == q, 0.0, part[g])
                part[g] = kept - column * row
        done = jnp.concatenate(part, 0)
        pivots = jnp.sum(jnp.where(i128 == j128, done, 0.0), axis=1, keepdims=True)
        scale = lax.rsqrt(pivots)
        scale = scale * (1.5 - 0.5 * pivots * scale * scale)
        own = jnp.where(i128 > j128, done, jnp.where(i128 == j128, 1.0, 0.0)) * scale
        across = dot(own, z_ref[pl.ds(at, 128), :])
        left = jnp.concatenate([own] * (n // 128), 1)
        inside = (col_b >= at) & (col_b < at + 128)
        across = jnp.where(inside, left, across)
        x_ref[pl.ds(at, 128), :] = jnp.where(col_b < at + 128, across, 0.0)
        down = z_ref[:, pl.ds(at, 128)]
        down = dot(jnp.where(row_n >= at + 128, down, 0.0), own, 1, 1)
        z = z_ref[...]
        z = jnp.where((col_n >= at) & (col_n < at + 128) & (row_nn >= at + 128), 0.0, z)
        z_ref[...] = z - dot(down, across)
        return 0

    lax.fori_loop(0, n // 128, block, 0)


def factor_inverse(gram):
    n = gram.shape[0]
    return pl.pallas_call(
        factor_kernel,
        out_shape=jax.ShapeDtypeStruct((n, n), jnp.float32),
        in_specs=[VMEM],
        out_specs=VMEM,
        scratch_shapes=[pltpu.VMEM((n, n), jnp.float32)],
        cost_estimate=pl.CostEstimate(flops=n * n * n * 20, bytes_accessed=n * n * 8, transcendentals=0),
    )(gram)


def exchanged(blocks, axis):
    return lax.all_to_all(blocks, axis, 0, 0, tiled=False)


def everywhere(block, axis, size):
    return exchanged(jnp.broadcast_to(block[None], (size,) + block.shape), axis)


def local(initial_carry, forcing, transition, partials, arc_of_row, counts):
    f32 = jnp.float32
    x, z = lax.axis_index("x"), lax.axis_index("z")
    p = lax.axis_index(("y", "core"))
    width = initial_carry.shape[1]
    rows = partials.shape[1]
    blocks = transition.shape[0]
    maps = transition[:, :, :, :, None] * jnp.eye(ARCS, dtype=f32)
    maps = maps.transpose(0, 1, 3, 2, 4).reshape(blocks, S, S)

    packed = call(offsets_kernel, jax.ShapeDtypeStruct((Z, PACK, 128), f32), 2, (10**8, 10**6))(maps, forcing)
    received = exchanged(packed, "z")
    total = call(totals_kernel, jax.ShapeDtypeStruct((PACK, 128), f32), 1, (10**7, 10**5))(received)
    totals = everywhere(total, "x", X)
    start = lax.dynamic_slice(initial_carry, (0, z * 128), (S, 128))
    incoming = call(incoming_kernel, jax.ShapeDtypeStruct((Z, S, 128), f32), 4, (10**7, 10**5), (0,))(
        x.reshape(1), totals, received, start
    )
    incoming = exchanged(incoming, "z")
    matrix = call(design_kernel, jax.ShapeDtypeStruct((rows, width), f32), 6, (10**8, 10**6), (0,))(
        counts, incoming, maps, forcing, partials, arc_of_row[None, :]
    )

    both = ("y", "core")
    panel = matrix[:, :PANEL]
    right = lax.ppermute(panel, both, [(0, 2)])
    left = lax.ppermute(panel, both, [(0, 6)])
    panel = jnp.where(p == 2, right, jnp.where(p == 6, left, panel))
    far = lax.ppermute(panel, both, [(2, 4)])
    panel = jnp.where(p == 4, far, panel)
    other = lax.ppermute(panel, both, [(0, 1), (2, 3), (4, 5), (6, 7)])
    panel = jnp.where(lax.axis_index("core") == 1, other, panel)

    share = PANEL // (Y * C)
    own = lax.dynamic_slice(panel, (0, p * share), (rows, share))
    products = dot(panel, jnp.concatenate([matrix, own], 1), 0, 0)
    wide = width + share
    products = exchanged(products.reshape(X, PANEL // X, wide), "x").sum(0)
    products = exchanged(products.reshape(Z, PANEL // X // Z, wide), "z").sum(0)
    products = everywhere(products, "z", Z).reshape(PANEL // X, wide)
    products = everywhere(products, "x", X).reshape(PANEL, wide)
    gram = everywhere(products[:, width:], both, Y * C)
    gram = gram.transpose(1, 0, 2).reshape(PANEL, PANEL)
    products = products[:, :width]

    inverse = factor_inverse(gram)
    row_block = dot(inverse, products)
    orthonormal = dot(panel, inverse, 1, 1)
    updated = matrix - dot(orthonormal, row_block)
    root_rows = math.sqrt(X * Z * rows)
    head = jnp.where(p == 0, orthonormal * root_rows, updated[:, :PANEL])
    return jnp.concatenate([head, updated[:, PANEL:]], 1), row_block / root_rows


def solution(mesh):
    mesh = Mesh(mesh.devices.reshape(X, Z, Y, C), ("x", "z", "y", "core"))
    e, q = ("x", "z"), ("y", "core")
    return jax.shard_map(
        local,
        mesh=mesh,
        in_specs=(P(None, q), P(e, None, q), P(e, None, None, None), P(None, e), P(e), P(e)),
        out_specs=(P(e, q), P(None, q)),
        check_vma=False,
    )
```

```python
import math

import jax
import jax.numpy as jnp
from jax import lax
from jax.experimental import pallas as pl
from jax.experimental.pallas import tpu as pltpu
from jax.sharding import Mesh
from jax.sharding import PartitionSpec as P


PANEL = 512
X, Z, Y, C = 4, 8, 4, 2
STATE, ARCS = 6, 8
S = STATE * ARCS
PACK = S + 8
HI = lax.Precision.HIGHEST
VMEM = pl.BlockSpec(memory_space=pltpu.VMEM)
SMEM = pl.BlockSpec(memory_space=pltpu.SMEM)


def call(kernel, out, n, cost, smem=()):
    flops, size = cost
    return pl.pallas_call(
        kernel,
        out_shape=out,
        in_specs=[SMEM if i in smem else VMEM for i in range(n)],
        out_specs=VMEM if not isinstance(out, (tuple, list)) else [VMEM] * len(out),
        cost_estimate=pl.CostEstimate(flops=flops, bytes_accessed=size, transcendentals=0),
    )


def dot(a, b, ca=1, cb=0):
    return lax.dot_general(a, b, (((ca,), (cb,)), ((), ())), precision=HI, preferred_element_type=jnp.float32)


def coefficients(tile):
    spread = lambda k: jnp.broadcast_to(tile[:, k : k + 1], (ARCS, 128))
    return [[spread(c * STATE + d) for d in range(STATE)] for c in range(STATE)]


def moved(coefficient, parts):
    out = []
    for row in coefficient:
        total = row[0] * parts[0]
        for d in range(1, STATE):
            total = total + row[d] * parts[d]
        out.append(total)
    return out


def split(value):
    return [value[c * ARCS : (c + 1) * ARCS] for c in range(STATE)]


def opened(tile):
    return [tile] + [pltpu.roll(tile, 128 - c * STATE, 1) for c in range(1, STATE)]


def closed(parts):
    lane = lax.broadcasted_iota(jnp.int32, (ARCS, 128), 1)
    parts = [jnp.where(lane < STATE, part, 0.0) for part in parts]
    out = parts[0]
    for c in range(1, STATE):
        out = out + pltpu.roll(parts[c], c * STATE, 1)
    return out


def offsets_kernel(d_ref, f_ref, o_ref):
    forced = lambda j, z: split(f_ref[j, :, z * 128 : (z + 1) * 128].astype(jnp.float32))
    whole = opened(d_ref[0])
    for j in range(1, d_ref.shape[0]):
        coefficient = coefficients(d_ref[j])
        for z in range(Z):
            parts = forced(0, z) if j == 1 else split(o_ref[z, :S, :])
            parts = moved(coefficient, parts)
            o_ref[z, :S, :] = jnp.concatenate([u + v for u, v in zip(parts, forced(j, z))], 0)
        whole = moved(coefficient, whole)
    whole = closed(whole)
    for z in range(Z):
        o_ref[z, S:, :] = whole


def totals_kernel(r_ref, o_ref):
    total = split(r_ref[0, :S, :])
    whole = opened(r_ref[0, S:, :])
    for z in range(1, Z):
        coefficient = coefficients(r_ref[z, S:, :])
        total = [u + v for u, v in zip(moved(coefficient, total), split(r_ref[z, :S, :]))]
        whole = moved(coefficient, whole)
    o_ref[:S, :] = jnp.concatenate(total, 0)
    o_ref[S:, :] = closed(whole)


def incoming_kernel(at_ref, t1, t2, t3, r_ref, i_ref, o_ref):
    x = at_ref[0]
    carry = split(i_ref[:, pl.ds(pl.multiple_of(at_ref[1] * 128, 128), 128)])
    for s, ref in ((3, t3), (2, t2), (1, t1)):
        after = moved(coefficients(ref[S:, :]), carry)
        carry = [jnp.where(s <= x, u + v, w) for u, v, w in zip(after, split(ref[:S, :]), carry)]
    for z in range(Z):
        o_ref[z] = jnp.concatenate(carry, 0)
        if z < Z - 1:
            after = moved(coefficients(r_ref[z, S:, :]), carry)
            carry = [u + v for u, v in zip(after, split(r_ref[z, :S, :]))]


def design_kernel(n_ref, i_ref, d_ref, f_ref, p_ref, a_ref, o_ref, h_ref, c_ref):
    blocks = d_ref.shape[0]
    rows = p_ref.shape[1]
    length = rows // blocks
    lane = lax.broadcasted_iota(jnp.int32, (ARCS, rows), 1)
    arc = lax.broadcasted_iota(jnp.int32, (ARCS, rows), 0)
    chosen = arc == a_ref[...]
    weights = []
    for j in range(blocks):
        live = (lane >= j * length) & (lane < j * length + jnp.minimum(n_ref[j], length)) & chosen
        for c in range(STATE):
            weights.append(jnp.where(live, p_ref[c : c + 1, :], 0.0))
    weights = jnp.concatenate(weights, 0)
    for j in range(blocks):
        coefficient = coefficients(d_ref[j])
        for z in range(Z):
            at = slice(z * 128, (z + 1) * 128)
            before = i_ref[z] if j == 0 else c_ref[(j - 1) * S : j * S, at]
            parts = zip(moved(coefficient, split(before)), split(f_ref[j, :, at].astype(jnp.float32)))
            c_ref[j * S : (j + 1) * S, at] = jnp.concatenate([u + v for u, v in parts], 0)
    out = dot(weights, c_ref[...], 0, 0)
    o_ref[...] = out
    h_ref[...] = out[:, :PANEL]


def first_factor_kernel(at_ref, g_ref, m_ref, x_ref, z_ref):
    n = z_ref.shape[0]
    half = n // C
    for c in range(C):
        source = m_ref if c else g_ref
        row = pl.multiple_of(lax.rem(at_ref[3] + c, C) * half, half)
        for u in range(Y):
            column = pl.multiple_of(lax.rem(at_ref[2] + Y - u, Y) * 128, 128)
            z_ref[pl.ds(row, half), pl.ds(column, 128)] = source[u]
    factor_blocks(0, 2, x_ref, z_ref)


def second_factor_kernel(z_in, x_in, x_ref, z_ref):
    z_ref[...] = z_in[...]
    x_ref[: PANEL // 2] = x_in[...]
    factor_blocks(2, 4, x_ref, z_ref)


def factor_blocks(first_block, end_block, x_ref, z_ref):
    n = z_ref.shape[0]
    sub = lax.broadcasted_iota(jnp.int32, (8, 128), 0)
    lane = lax.broadcasted_iota(jnp.int32, (8, 128), 1)
    row_n = lax.broadcasted_iota(jnp.int32, (n, 128), 0)
    col_n = lax.broadcasted_iota(jnp.int32, (n, n), 1)
    row_nn = lax.broadcasted_iota(jnp.int32, (n, n), 0)
    col_b = lax.broadcasted_iota(jnp.int32, (128, n), 1)
    i128 = lax.broadcasted_iota(jnp.int32, (128, 128), 0)
    j128 = lax.broadcasted_iota(jnp.int32, (128, 128), 1)
    wide = lambda v: jnp.broadcast_to(v, (1, 128))
    tile = lambda v: jnp.broadcast_to(v, (8, 128))

    def block(k, _):
        at = pl.multiple_of(k * 128, 128)
        part = [z_ref[pl.ds(at + 8 * g, 8), pl.ds(at, 128)] for g in range(16)]
        for q in range(0, 128, 2):
            gq, sq = q // 8, q % 8
            first, second = part[gq][sq : sq + 1, :], part[gq][sq + 1 : sq + 2, :]
            a, b, c = wide(first[:, q : q + 1]), wide(second[:, q : q + 1]), wide(second[:, q + 1 : q + 2])
            inverse = 1.0 / (a * c - b * b)
            l1 = lane[:1]
            one = jnp.where(l1 == q, c, jnp.where(l1 == q + 1, -b, c * first - b * second)) * inverse
            two = jnp.where(l1 == q, -b, jnp.where(l1 == q + 1, a, a * second - b * first)) * inverse
            one, two = tile(one), tile(two)
            pair = (lane == q) | (lane == q + 1)
            for g in range(gq, 16):
                if g == gq and sq == 6:
                    continue
                left, right = tile(part[g][:, q : q + 1]), tile(part[g][:, q + 1 : q + 2])
                if g == gq:
                    below = sub > sq + 1
                    left, right = jnp.where(below, left, 0.0), jnp.where(below, right, 0.0)
                    kept = jnp.where(pair & below, 0.0, part[g])
                else:
                    kept = jnp.where(pair, 0.0, part[g])
                part[g] = (kept - left * one) - right * two
        done = jnp.concatenate(part, 0)
        odd = lax.rem(i128, 2) == 1
        diag = jnp.sum(jnp.where(i128 == j128, done, 0.0), axis=1, keepdims=True)
        beside = jnp.sum(jnp.where((j128 == i128 - 1) & odd, done, 0.0), axis=1, keepdims=True)
        unit = jnp.where(i128 == j128, 1.0, jnp.where(j128 < i128 - jnp.where(odd, 1, 0), done, 0.0))
        above = pltpu.roll(unit, 1, 0)
        ratio = jnp.where(odd[:, :1], beside / pltpu.roll(diag, 1, 0), 0.0)
        unit = unit - ratio * above
        pivots = diag - ratio * beside
        scale = lax.rsqrt(pivots)
        scale = scale * (1.5 - 0.5 * pivots * scale * scale)
        own = unit * scale
        across = dot(own, z_ref[pl.ds(at, 128), :])
        left = jnp.concatenate([own] * (n // 128), 1)
        inside = (col_b >= at) & (col_b < at + 128)
        across = jnp.where(inside, left, across)
        x_ref[pl.ds(at, 128), :] = jnp.where(col_b < at + 128, across, 0.0)
        down = z_ref[:, pl.ds(at, 128)]
        down = dot(jnp.where(row_n >= at + 128, down, 0.0), own, 1, 1)
        z = z_ref[...]
        z = jnp.where((col_n >= at) & (col_n < at + 128) & (row_nn >= at + 128), 0.0, z)
        z_ref[...] = z - dot(down, across)
        return 0

    lax.fori_loop(first_block, end_block, block, 0)


def factor_start(at, gram, mate):
    n = PANEL
    return pl.pallas_call(
        first_factor_kernel,
        out_shape=[jax.ShapeDtypeStruct((n // 2, n), jnp.float32), jax.ShapeDtypeStruct((n, n), jnp.float32)],
        in_specs=[SMEM, VMEM, VMEM],
        out_specs=[VMEM, VMEM],
        cost_estimate=pl.CostEstimate(flops=2 * 10**10, bytes_accessed=n * n * 8, transcendentals=0),
    )(at, gram, mate)


def factor_end(z, x):
    n = PANEL
    return pl.pallas_call(
        second_factor_kernel,
        out_shape=jax.ShapeDtypeStruct((n, n), jnp.float32),
        in_specs=[VMEM, VMEM],
        out_specs=VMEM,
        scratch_shapes=[pltpu.VMEM((n, n), jnp.float32)],
        cost_estimate=pl.CostEstimate(flops=2 * 10**10, bytes_accessed=n * n * 8, transcendentals=0),
    )(z, x)


def final_kernel(at_ref, l_ref, p_ref, m_ref, a_ref, b0, b1, b2, b3, o_ref, r_ref, ga_ref, gb_ref):
    root = math.sqrt(X * Z * p_ref.shape[0])
    x, p = at_ref[0], at_ref[2] * C + at_ref[3]
    mid, width = ga_ref.shape[1], m_ref.shape[1]
    step = PANEL // X
    tile = step // Z
    inverse = l_ref[...]
    basis = dot(p_ref[...], inverse, 1, 1)
    for s, ref in enumerate((b0, b1, b2, b3)):
        row = pl.multiple_of(lax.rem(x + X - s, X) * step, step)
        gb_ref[pl.ds(row, step), :] = ref[...]
        for z in range(Z):
            ga_ref[pl.ds(pl.multiple_of(row + z * tile, tile), tile), :] = a_ref[z, s]
    for lo, hi, source in ((0, mid, ga_ref), (mid, width, gb_ref)):
        rows = dot(inverse, source[...])
        r_ref[:, lo:hi] = rows * (1.0 / root)
        updated = m_ref[:, lo:hi] - dot(basis, rows)
        cut = min(hi, PANEL) - lo
        if cut > 0:
            o_ref[:, lo : lo + cut] = jnp.where(p == 0, basis[:, lo : lo + cut] * root, updated[:, :cut])
            if lo + cut < hi:
                o_ref[:, lo + cut : hi] = updated[:, cut:]
        else:
            o_ref[:, lo:hi] = updated


def exchanged(blocks, axis):
    return lax.all_to_all(blocks, axis, 0, 0, tiled=False)


def everywhere(block, axis, size):
    return exchanged(jnp.broadcast_to(block[None], (size,) + block.shape), axis)


def shift(block, axis, size, by):
    return lax.ppermute(block, axis, [(i, (i + by) % size) for i in range(size)])


def collected(block, axis, size):
    return jnp.stack([block] + [shift(block, axis, size, k) for k in range(1, size)], 0)


def local(initial_carry, forcing, transition, partials, arc_of_row, counts):
    f32 = jnp.float32
    x, z = lax.axis_index("x"), lax.axis_index("z")
    p = lax.axis_index(("y", "core"))
    width = initial_carry.shape[1]
    rows = partials.shape[1]
    blocks = transition.shape[0]
    core, y = lax.axis_index("core"), lax.axis_index("y")
    at = jnp.stack([x, z, y, core])
    maps = transition.transpose(0, 3, 1, 2).reshape(blocks, ARCS, STATE * STATE)
    maps = jnp.pad(maps, ((0, 0), (0, 0), (0, 128 - STATE * STATE)))

    packed = call(offsets_kernel, jax.ShapeDtypeStruct((Z, PACK, 128), f32), 2, (10**7, 10**6))(maps, forcing)
    received = exchanged(packed, "z")
    total = call(totals_kernel, jax.ShapeDtypeStruct((PACK, 128), f32), 1, (10**6, 10**5))(received)
    totals = [shift(total, "x", X, k) for k in range(1, X)]
    incoming = call(incoming_kernel, jax.ShapeDtypeStruct((Z, S, 128), f32), 6, (10**6, 10**5), (0,))(
        at, *totals, received, initial_carry
    )
    incoming = exchanged(incoming, "z")
    matrix, panel = pl.pallas_call(
        design_kernel,
        out_shape=[jax.ShapeDtypeStruct((rows, width), f32), jax.ShapeDtypeStruct((rows, PANEL), f32)],
        in_specs=[SMEM] + [VMEM] * 5,
        out_specs=[VMEM, VMEM],
        scratch_shapes=[pltpu.VMEM((blocks * S, width), f32)],
        cost_estimate=pl.CostEstimate(flops=10**8, bytes_accessed=10**6, transcendentals=0),
    )(counts, incoming, maps, forcing, partials, arc_of_row[None, :])

    both = ("y", "core")
    right = lax.ppermute(panel, both, [(0, 2)])
    left = lax.ppermute(panel, both, [(0, 6)])
    panel = jnp.where(p == 2, right, jnp.where(p == 6, left, panel))
    far = lax.ppermute(panel, both, [(2, 4)])
    panel = jnp.where(p == 4, far, panel)
    other = lax.ppermute(panel, both, [(0, 1), (2, 3), (4, 5), (6, 7)])
    panel = jnp.where(lax.axis_index("core") == 1, other, panel)

    half, quarter, step = PANEL // C, PANEL // Y, PANEL // X
    tile, mid = step // Z, 3 * width // 8
    gram = dot(
        lax.dynamic_slice(panel, (0, core * half), (rows, half)),
        lax.dynamic_slice(panel, (0, y * quarter), (rows, quarter)),
        0, 0,
    )
    gram, panel = lax.optimization_barrier((gram, panel))
    gram = exchanged(gram.reshape(X * Z, half // X // Z, quarter), ("x", "z"))
    gram = gram.sum(0)
    turned = lax.dynamic_slice(jnp.concatenate([panel, panel], 1), (0, x * step), (rows, PANEL))
    far, near, last, own = [dot(turned[:, k * step : (k + 1) * step], matrix, 0, 0) for k in (2, 1, 3, 0)]
    right, left = shift(far[:, : width // 2], "x", X, 1), shift(far[:, width // 2 :], "x", X, -1)
    right = jnp.concatenate([near[:, : width // 2] + right, near[:, width // 2 :]], 1)
    left = jnp.concatenate([last[:, : width // 2], last[:, width // 2 :] + left], 1)
    products = own + shift(right, "x", X, 1) + shift(left, "x", X, -1)

    gram = everywhere(gram, ("x", "z"), X * Z).reshape(half, quarter)
    gram, products = lax.optimization_barrier((gram, products))
    gram = collected(gram, "y", Y)
    mate = lax.ppermute(gram, "core", [(0, 1), (1, 0)])

    products = exchanged(products.reshape(Z, tile, width), "z").sum(0)
    a, b = products[:, :mid], products[:, mid:]
    b = everywhere(b, "z", Z).reshape(step, width - mid)
    a = collected(a, "x", X)
    a = everywhere(a, "z", Z)
    b = [b] + [shift(b, "x", X, k) for k in range(1, X)]

    upper, rest = factor_start(at, gram, mate)
    inverse = factor_end(rest, upper)
    return pl.pallas_call(
        final_kernel,
        out_shape=[jax.ShapeDtypeStruct((rows, width), f32), jax.ShapeDtypeStruct((PANEL, width), f32)],
        in_specs=[SMEM] + [VMEM] * 8,
        out_specs=[VMEM, VMEM],
        scratch_shapes=[pltpu.VMEM((PANEL, mid), f32), pltpu.VMEM((PANEL, width - mid), f32)],
        cost_estimate=pl.CostEstimate(flops=4 * 10**9, bytes_accessed=6 * 10**6, transcendentals=0),
    )(at, inverse, panel, matrix, a, *b)


def solution(mesh):
    mesh = Mesh(mesh.devices.reshape(X, Z, Y, C), ("x", "z", "y", "core"))
    e, q = ("x", "z"), ("y", "core")
    return jax.shard_map(
        local,
        mesh=mesh,
        in_specs=(P(None, q), P(e, None, q), P(e, None, None, None), P(None, e), P(e), P(e)),
        out_specs=(P(e, q), P(None, q)),
        check_vma=False,
    )
```

```python
import math

import jax
import jax.numpy as jnp
from jax import lax
from jax.experimental import pallas as pl
from jax.experimental.pallas import tpu as pltpu
from jax.sharding import Mesh
from jax.sharding import PartitionSpec as P


PANEL = 512
X, Z, Y, C = 4, 8, 4, 2
STATE, ARCS = 6, 8
S = STATE * ARCS
PACK = S + 8
LIMIT = 12 * 2**20
HI = lax.Precision.HIGHEST
VMEM = pl.BlockSpec(memory_space=pltpu.VMEM)
SMEM = pl.BlockSpec(memory_space=pltpu.SMEM)


def call(kernel, out, n, cost, smem=()):
    flops, size = cost
    return pl.pallas_call(
        kernel,
        out_shape=out,
        in_specs=[SMEM if i in smem else VMEM for i in range(n)],
        out_specs=VMEM if not isinstance(out, (tuple, list)) else [VMEM] * len(out),
        compiler_params=pltpu.CompilerParams(vmem_limit_bytes=LIMIT),
        cost_estimate=pl.CostEstimate(flops=flops, bytes_accessed=size, transcendentals=0),
    )


def dot(a, b, ca=1, cb=0):
    return lax.dot_general(a, b, (((ca,), (cb,)), ((), ())), precision=HI, preferred_element_type=jnp.float32)


def coefficients(tile):
    spread = lambda k: jnp.broadcast_to(tile[:, k : k + 1], (ARCS, 128))
    return [[spread(c * STATE + d) for d in range(STATE)] for c in range(STATE)]


def moved(coefficient, parts):
    out = []
    for row in coefficient:
        total = row[0] * parts[0]
        for d in range(1, STATE):
            total = total + row[d] * parts[d]
        out.append(total)
    return out


def split(value):
    return [value[c * ARCS : (c + 1) * ARCS] for c in range(STATE)]


def opened(tile):
    return [tile] + [pltpu.roll(tile, 128 - c * STATE, 1) for c in range(1, STATE)]


def closed(parts):
    lane = lax.broadcasted_iota(jnp.int32, (ARCS, 128), 1)
    parts = [jnp.where(lane < STATE, part, 0.0) for part in parts]
    out = parts[0]
    for c in range(1, STATE):
        out = out + pltpu.roll(parts[c], c * STATE, 1)
    return out


def offsets_kernel(d_ref, f_ref, o_ref):
    forced = lambda j, z: split(f_ref[j, :, z * 128 : (z + 1) * 128].astype(jnp.float32))
    whole = opened(d_ref[0])
    for j in range(1, d_ref.shape[0]):
        coefficient = coefficients(d_ref[j])
        for z in range(Z):
            parts = forced(0, z) if j == 1 else split(o_ref[z, :S, :])
            parts = moved(coefficient, parts)
            o_ref[z, :S, :] = jnp.concatenate([u + v for u, v in zip(parts, forced(j, z))], 0)
        whole = moved(coefficient, whole)
    whole = closed(whole)
    for z in range(Z):
        o_ref[z, S:, :] = whole


def totals_kernel(r_ref, o_ref):
    total = split(r_ref[0, :S, :])
    whole = opened(r_ref[0, S:, :])
    for z in range(1, Z):
        coefficient = coefficients(r_ref[z, S:, :])
        total = [u + v for u, v in zip(moved(coefficient, total), split(r_ref[z, :S, :]))]
        whole = moved(coefficient, whole)
    o_ref[:S, :] = jnp.concatenate(total, 0)
    o_ref[S:, :] = closed(whole)


def incoming_kernel(at_ref, t1, t2, t3, r_ref, i_ref, o_ref):
    x = at_ref[0]
    carry = split(i_ref[:, pl.ds(pl.multiple_of(at_ref[1] * 128, 128), 128)])
    for s, ref in ((3, t3), (2, t2), (1, t1)):
        after = moved(coefficients(ref[S:, :]), carry)
        carry = [jnp.where(s <= x, u + v, w) for u, v, w in zip(after, split(ref[:S, :]), carry)]
    for z in range(Z):
        o_ref[z] = jnp.concatenate(carry, 0)
        if z < Z - 1:
            after = moved(coefficients(r_ref[z, S:, :]), carry)
            carry = [u + v for u, v in zip(after, split(r_ref[z, :S, :]))]


def design_kernel(n_ref, i_ref, d_ref, f_ref, p_ref, a_ref, o_ref, h_ref, c_ref):
    blocks = d_ref.shape[0]
    rows = p_ref.shape[1]
    length = rows // blocks
    lane = lax.broadcasted_iota(jnp.int32, (ARCS, rows), 1)
    arc = lax.broadcasted_iota(jnp.int32, (ARCS, rows), 0)
    chosen = arc == a_ref[...]
    weights = []
    for j in range(blocks):
        live = (lane >= j * length) & (lane < j * length + jnp.minimum(n_ref[j], length)) & chosen
        for c in range(STATE):
            weights.append(jnp.where(live, p_ref[c : c + 1, :], 0.0))
    weights = jnp.concatenate(weights, 0)
    for j in range(blocks):
        coefficient = coefficients(d_ref[j])
        for z in range(Z):
            at = slice(z * 128, (z + 1) * 128)
            before = i_ref[z] if j == 0 else c_ref[(j - 1) * S : j * S, at]
            parts = zip(moved(coefficient, split(before)), split(f_ref[j, :, at].astype(jnp.float32)))
            c_ref[j * S : (j + 1) * S, at] = jnp.concatenate([u + v for u, v in parts], 0)
    out = dot(weights, c_ref[...], 0, 0)
    o_ref[...] = out
    h_ref[...] = out[:, :PANEL]


def first_factor_kernel(at_ref, g_ref, m_ref, x_ref, o_ref, z_ref):
    n = z_ref.shape[0]
    half = n // C
    for c in range(C):
        source = m_ref if c else g_ref
        row = pl.multiple_of(lax.rem(at_ref[3] + c, C) * half, half)
        for u in range(Y):
            column = pl.multiple_of(lax.rem(at_ref[2] + Y - u, Y) * 128, 128)
            z_ref[pl.ds(row, half), pl.ds(column, 128)] = source[u]
    factor_block(0, x_ref, z_ref, 0, o_ref)


def second_factor_kernel(z_ref, x_ref, o_ref):
    factor_block(1, x_ref, z_ref, 128, o_ref)


def last_factor_kernel(z_ref, x_ref, y_ref, o_ref):
    factor_block(2, x_ref, z_ref, 256, o_ref)
    factor_block(3, y_ref, o_ref, 384, None)


def factor_block(k, x_ref, z_ref, top, o_ref):
    lo, hi = k * 128, k * 128 + 128
    sub = lax.broadcasted_iota(jnp.int32, (8, 128), 0)
    lane = lax.broadcasted_iota(jnp.int32, (8, 128), 1)
    i128 = lax.broadcasted_iota(jnp.int32, (128, 128), 0)
    j128 = lax.broadcasted_iota(jnp.int32, (128, 128), 1)
    wide = lambda v: jnp.broadcast_to(v, (1, 128))
    tile = lambda v: jnp.broadcast_to(v, (8, 128))
    here = slice(lo - top, hi - top)
    block = z_ref[here, lo:hi]
    part = [block[8 * g : 8 * g + 8] for g in range(16)]
    for q in range(0, 128, 2):
        gq, sq = q // 8, q % 8
        first, second = part[gq][sq : sq + 1, :], part[gq][sq + 1 : sq + 2, :]
        a, b, c = wide(first[:, q : q + 1]), wide(second[:, q : q + 1]), wide(second[:, q + 1 : q + 2])
        inverse = 1.0 / (a * c - b * b)
        l1 = lane[:1]
        one = jnp.where(l1 == q, c, jnp.where(l1 == q + 1, -b, c * first - b * second)) * inverse
        two = jnp.where(l1 == q, -b, jnp.where(l1 == q + 1, a, a * second - b * first)) * inverse
        one, two = tile(one), tile(two)
        pair = (lane == q) | (lane == q + 1)
        for g in range(gq, 16):
            if g == gq and sq == 6:
                continue
            left, right = tile(part[g][:, q : q + 1]), tile(part[g][:, q + 1 : q + 2])
            if g == gq:
                below = sub > sq + 1
                left, right = jnp.where(below, left, 0.0), jnp.where(below, right, 0.0)
                kept = jnp.where(pair & below, 0.0, part[g])
            else:
                kept = jnp.where(pair, 0.0, part[g])
            part[g] = (kept - left * one) - right * two
    done = jnp.concatenate(part, 0)
    odd = lax.rem(i128, 2) == 1
    diag = jnp.sum(jnp.where(i128 == j128, done, 0.0), axis=1, keepdims=True)
    beside = jnp.sum(jnp.where((j128 == i128 - 1) & odd, done, 0.0), axis=1, keepdims=True)
    unit = jnp.where(i128 == j128, 1.0, jnp.where(j128 < i128 - jnp.where(odd, 1, 0), done, 0.0))
    above = pltpu.roll(unit, 1, 0)
    ratio = jnp.where(odd[:, :1], beside / pltpu.roll(diag, 1, 0), 0.0)
    unit = unit - ratio * above
    pivots = diag - ratio * beside
    scale = lax.rsqrt(pivots)
    scale = scale * (1.5 - 0.5 * pivots * scale * scale)
    own = unit * scale
    x_ref[:, lo:hi] = own
    if lo:
        left = dot(own, z_ref[here, :lo])
        x_ref[:, :lo] = left
    if hi < PANEL:
        down = dot(z_ref[hi - top :, lo:hi], own, 1, 1)
        if lo:
            o_ref[:, :lo] = z_ref[hi - top :, :lo] - dot(down, left)
        o_ref[:, lo:hi] = -dot(down, own)
        o_ref[:, hi:] = z_ref[hi - top :, hi:] - dot(down, dot(own, z_ref[here, hi:]))


def factor_inverse(at, gram, mate):
    n = PANEL
    shape = lambda r, c: jax.ShapeDtypeStruct((r, c), jnp.float32)
    step = lambda kernel, out, ins, scratch, k: pl.pallas_call(
        kernel,
        out_shape=out,
        in_specs=ins,
        out_specs=[VMEM] * len(out),
        scratch_shapes=scratch,
        compiler_params=pltpu.CompilerParams(vmem_limit_bytes=LIMIT),
        cost_estimate=pl.CostEstimate(flops=k * 10**10, bytes_accessed=n * n * 4, transcendentals=0),
    )
    square = [pltpu.VMEM((n, n), jnp.float32)]
    l0, z = step(first_factor_kernel, [shape(128, 128), shape(384, n)], [SMEM, VMEM, VMEM], square, 1)(at, gram, mate)
    l1, z = step(second_factor_kernel, [shape(128, 256), shape(256, n)], [VMEM], [], 1)(z)
    rest = [pltpu.VMEM((128, n), jnp.float32)]
    l2, l3 = step(last_factor_kernel, [shape(128, 384), shape(128, n)], [VMEM], rest, 2)(z)
    return l0, l1, l2, l3


def final_kernel(at_ref, l0, l1, l2, l3, p_ref, m_ref, a_ref, b0, b1, b2, b3, o_ref, r_ref, g_ref, q_ref):
    root = math.sqrt(X * Z * p_ref.shape[0])
    x, p = at_ref[0], at_ref[2] * C + at_ref[3]
    mid, width = a_ref.shape[3], m_ref.shape[1]
    step = PANEL // X
    tile = step // Z
    inverse = [l0[...], l1[...], l2[...], l3[...]]
    basis = [dot(p_ref[:, : row.shape[1]], row, 1, 1) for row in inverse]
    q_ref[...] = jnp.concatenate(basis, 1)
    for s, ref in enumerate((b0, b1, b2, b3)):
        row = pl.multiple_of(lax.rem(x + X - s, X) * step, step)
        g_ref[pl.ds(row, step), mid:] = ref[...]
        for z in range(Z):
            g_ref[pl.ds(pl.multiple_of(row + z * tile, tile), tile), :mid] = a_ref[z, s]

    def columns(t, _):
        at = pl.ds(pl.multiple_of(t * 256, 256), 256)
        rows = jnp.concatenate([dot(l[...], g_ref[: l.shape[1], at]) for l in (l0, l1, l2, l3)], 0)
        r_ref[:, at] = rows * (1.0 / root)
        updated = m_ref[:, at] - dot(q_ref[...], rows)
        head = q_ref[:, pl.ds(pl.multiple_of(lax.rem(t, PANEL // 256) * 256, 256), 256)] * root
        o_ref[:, at] = jnp.where((p == 0) & (t < PANEL // 256), head, updated)
        return 0

    lax.fori_loop(0, width // 256, columns, 0)


def exchanged(blocks, axis):
    return lax.all_to_all(blocks, axis, 0, 0, tiled=False)


def everywhere(block, axis, size):
    return exchanged(jnp.broadcast_to(block[None], (size,) + block.shape), axis)


def shift(block, axis, size, by):
    return lax.ppermute(block, axis, [(i, (i + by) % size) for i in range(size)])


def collected(block, axis, size):
    return jnp.stack([block] + [shift(block, axis, size, k) for k in range(1, size)], 0)


def local(initial_carry, forcing, transition, partials, arc_of_row, counts):
    f32 = jnp.float32
    x, z = lax.axis_index("x"), lax.axis_index("z")
    p = lax.axis_index(("y", "core"))
    width = initial_carry.shape[1]
    rows = partials.shape[1]
    blocks = transition.shape[0]
    core, y = lax.axis_index("core"), lax.axis_index("y")
    at = jnp.stack([x, z, y, core])
    maps = transition.transpose(0, 3, 1, 2).reshape(blocks, ARCS, STATE * STATE)
    maps = jnp.pad(maps, ((0, 0), (0, 0), (0, 128 - STATE * STATE)))

    packed = call(offsets_kernel, jax.ShapeDtypeStruct((Z, PACK, 128), f32), 2, (10**7, 10**6))(maps, forcing)
    received = exchanged(packed, "z")
    total = call(totals_kernel, jax.ShapeDtypeStruct((PACK, 128), f32), 1, (10**6, 10**5))(received)
    totals = [shift(total, "x", X, k) for k in range(1, X)]
    incoming = call(incoming_kernel, jax.ShapeDtypeStruct((Z, S, 128), f32), 6, (10**6, 10**5), (0,))(
        at, *totals, received, initial_carry
    )
    incoming = exchanged(incoming, "z")
    matrix, panel = pl.pallas_call(
        design_kernel,
        out_shape=[jax.ShapeDtypeStruct((rows, width), f32), jax.ShapeDtypeStruct((rows, PANEL), f32)],
        in_specs=[SMEM] + [VMEM] * 5,
        out_specs=[VMEM, VMEM],
        scratch_shapes=[pltpu.VMEM((blocks * S, width), f32)],
        compiler_params=pltpu.CompilerParams(vmem_limit_bytes=LIMIT),
        cost_estimate=pl.CostEstimate(flops=10**8, bytes_accessed=10**6, transcendentals=0),
    )(counts, incoming, maps, forcing, partials, arc_of_row[None, :])

    both = ("y", "core")
    right, far, left = [lax.ppermute(panel, both, [(0, k)]) for k in (2, 4, 6)]
    panel = jnp.where(p == 2, right, jnp.where(p == 4, far, jnp.where(p == 6, left, panel)))
    other = lax.ppermute(panel, both, [(0, 1), (2, 3), (4, 5), (6, 7)])
    panel = jnp.where(lax.axis_index("core") == 1, other, panel)

    half, quarter, step = PANEL // C, PANEL // Y, PANEL // X
    tile, mid = step // Z, width // 4
    gram = dot(
        lax.dynamic_slice(panel, (0, core * half), (rows, half)),
        lax.dynamic_slice(panel, (0, y * quarter), (rows, quarter)),
        0, 0,
    )
    gram, panel = lax.optimization_barrier((gram, panel))
    gram = exchanged(gram.reshape(X * Z, half // X // Z, quarter), ("x", "z"))
    gram = gram.sum(0)
    turned = lax.dynamic_slice(jnp.concatenate([panel, panel], 1), (0, x * step), (rows, PANEL))
    parts = [dot(turned[:, k * step : (k + 1) * step], matrix, 0, 0) for k in range(X)]
    sent = [shift(parts[k], "x", X, k) for k in (2, 1, 3)]
    gram = everywhere(gram, ("x", "z"), X * Z).reshape(half, quarter)
    gram, sent = lax.optimization_barrier((gram, sent))
    gram = [gram] + [shift(gram, "y", Y, k) for k in (1, 2, 3)]
    gram = jnp.stack(gram, 0)
    mate = lax.ppermute(gram, "core", [(0, 1), (1, 0)])

    products = parts[0] + sent[0] + sent[1] + sent[2]
    products = exchanged(products.reshape(Z, tile, width), "z")
    products = products.sum(0)
    a, b = products[:, :mid], products[:, mid:]
    b = everywhere(b, "z", Z)
    b = b.reshape(step, width - mid)
    a = collected(a, "x", X)
    a = everywhere(a, "z", Z)
    b = [b] + [shift(b, "x", X, k) for k in (1, 2, 3)]

    inverse = factor_inverse(at, gram, mate)
    return pl.pallas_call(
        final_kernel,
        out_shape=[jax.ShapeDtypeStruct((rows, width), f32), jax.ShapeDtypeStruct((PANEL, width), f32)],
        in_specs=[SMEM] + [VMEM] * 11,
        out_specs=[VMEM, VMEM],
        scratch_shapes=[pltpu.VMEM((PANEL, width), f32), pltpu.VMEM((rows, PANEL), f32)],
        compiler_params=pltpu.CompilerParams(vmem_limit_bytes=LIMIT),
        cost_estimate=pl.CostEstimate(flops=4 * 10**9, bytes_accessed=6 * 10**6, transcendentals=0),
    )(at, *inverse, panel, matrix, a, *b)


def solution(mesh):
    mesh = Mesh(mesh.devices.reshape(X, Z, Y, C), ("x", "z", "y", "core"))
    e, q = ("x", "z"), ("y", "core")
    return jax.shard_map(
        local,
        mesh=mesh,
        in_specs=(P(None, q), P(e, None, q), P(e, None, None, None), P(None, e), P(e), P(e)),
        out_specs=(P(e, q), P(None, q)),
        check_vma=False,
    )
```

```python
import functools
import math

import jax
import jax.numpy as jnp
from jax import lax
from jax.experimental import pallas as pl
from jax.experimental.pallas import tpu as pltpu
from jax.sharding import Mesh
from jax.sharding import PartitionSpec as P


PANEL = 512
X, Z, Y, C = 4, 8, 4, 2
STATE, ARCS = 6, 8
S = STATE * ARCS
PACK = S + 8
LIMIT = 12 * 2**20
HI = lax.Precision.HIGHEST
VMEM = pl.BlockSpec(memory_space=pltpu.VMEM)
SMEM = pl.BlockSpec(memory_space=pltpu.SMEM)


def call(kernel, out, n, cost, smem=()):
    flops, size = cost
    return pl.pallas_call(
        kernel,
        out_shape=out,
        in_specs=[SMEM if i in smem else VMEM for i in range(n)],
        out_specs=VMEM if not isinstance(out, (tuple, list)) else [VMEM] * len(out),
        compiler_params=pltpu.CompilerParams(vmem_limit_bytes=LIMIT),
        cost_estimate=pl.CostEstimate(flops=flops, bytes_accessed=size, transcendentals=0),
    )


def dot(a, b, ca=1, cb=0):
    return lax.dot_general(a, b, (((ca,), (cb,)), ((), ())), precision=HI, preferred_element_type=jnp.float32)


def coefficients(tile):
    spread = lambda k: jnp.broadcast_to(tile[:, k : k + 1], (ARCS, 128))
    return [[spread(c * STATE + d) for d in range(STATE)] for c in range(STATE)]


def moved(coefficient, parts):
    out = []
    for row in coefficient:
        total = row[0] * parts[0]
        for d in range(1, STATE):
            total = total + row[d] * parts[d]
        out.append(total)
    return out


def split(value):
    return [value[c * ARCS : (c + 1) * ARCS] for c in range(STATE)]


def opened(tile):
    return [tile] + [pltpu.roll(tile, 128 - c * STATE, 1) for c in range(1, STATE)]


def closed(parts):
    lane = lax.broadcasted_iota(jnp.int32, (ARCS, 128), 1)
    parts = [jnp.where(lane < STATE, part, 0.0) for part in parts]
    out = parts[0]
    for c in range(1, STATE):
        out = out + pltpu.roll(parts[c], c * STATE, 1)
    return out


def offsets_kernel(d_ref, f_ref, o_ref):
    forced = lambda j, z: split(f_ref[j, :, z * 128 : (z + 1) * 128].astype(jnp.float32))
    whole = opened(d_ref[0])
    for j in range(1, d_ref.shape[0]):
        coefficient = coefficients(d_ref[j])
        for z in range(Z):
            parts = forced(0, z) if j == 1 else split(o_ref[z, :S, :])
            parts = moved(coefficient, parts)
            o_ref[z, :S, :] = jnp.concatenate([u + v for u, v in zip(parts, forced(j, z))], 0)
        whole = moved(coefficient, whole)
    whole = closed(whole)
    for z in range(Z):
        o_ref[z, S:, :] = whole


def totals_kernel(r_ref, o_ref):
    total = split(r_ref[0, :S, :])
    whole = opened(r_ref[0, S:, :])
    for z in range(1, Z):
        coefficient = coefficients(r_ref[z, S:, :])
        total = [u + v for u, v in zip(moved(coefficient, total), split(r_ref[z, :S, :]))]
        whole = moved(coefficient, whole)
    o_ref[:S, :] = jnp.concatenate(total, 0)
    o_ref[S:, :] = closed(whole)


def incoming_kernel(at_ref, t1, t2, t3, r_ref, i_ref, o_ref):
    x = at_ref[0]
    carry = split(i_ref[:, pl.ds(pl.multiple_of(at_ref[1] * 128, 128), 128)])
    for s, ref in ((3, t3), (2, t2), (1, t1)):
        after = moved(coefficients(ref[S:, :]), carry)
        carry = [jnp.where(s <= x, u + v, w) for u, v, w in zip(after, split(ref[:S, :]), carry)]
    for z in range(Z):
        o_ref[z] = jnp.concatenate(carry, 0)
        if z < Z - 1:
            after = moved(coefficients(r_ref[z, S:, :]), carry)
            carry = [u + v for u, v in zip(after, split(r_ref[z, :S, :]))]


def design_kernel(n_ref, i_ref, d_ref, f_ref, p_ref, a_ref, o_ref, h_ref, c_ref):
    blocks = d_ref.shape[0]
    rows = p_ref.shape[1]
    length = rows // blocks
    lane = lax.broadcasted_iota(jnp.int32, (ARCS, rows), 1)
    arc = lax.broadcasted_iota(jnp.int32, (ARCS, rows), 0)
    chosen = arc == a_ref[...]
    weights = []
    for j in range(blocks):
        live = (lane >= j * length) & (lane < j * length + jnp.minimum(n_ref[j], length)) & chosen
        for c in range(STATE):
            weights.append(jnp.where(live, p_ref[c : c + 1, :], 0.0))
    weights = jnp.concatenate(weights, 0)
    for j in range(blocks):
        coefficient = coefficients(d_ref[j])
        for z in range(Z):
            at = slice(z * 128, (z + 1) * 128)
            before = i_ref[z] if j == 0 else c_ref[(j - 1) * S : j * S, at]
            parts = zip(moved(coefficient, split(before)), split(f_ref[j, :, at].astype(jnp.float32)))
            c_ref[j * S : (j + 1) * S, at] = jnp.concatenate([u + v for u, v in parts], 0)
    out = dot(weights, c_ref[...], 0, 0)
    o_ref[...] = out
    h_ref[...] = out[:, :PANEL]


def first_factor_kernel(at_ref, g_ref, m_ref, x_ref, o_ref, z_ref):
    n = z_ref.shape[0]
    half = n // C
    for c in range(C):
        source = m_ref if c else g_ref
        row = pl.multiple_of(lax.rem(at_ref[3] + c, C) * half, half)
        for u in range(Y):
            column = pl.multiple_of(lax.rem(at_ref[2] + Y - u, Y) * 128, 128)
            z_ref[pl.ds(row, half), pl.ds(column, 128)] = source[u]
    factor_block(0, x_ref, z_ref, 0, o_ref)


def second_factor_kernel(z_ref, x_ref, o_ref):
    factor_block(1, x_ref, z_ref, 128, o_ref)


def last_factor_kernel(z_ref, x_ref, y_ref, o_ref):
    factor_block(2, x_ref, z_ref, 256, o_ref)
    factor_block(3, y_ref, o_ref, 384, None)


def factor_block(k, x_ref, z_ref, top, o_ref):
    lo, hi = k * 128, k * 128 + 128
    sub = lax.broadcasted_iota(jnp.int32, (8, 128), 0)
    lane = lax.broadcasted_iota(jnp.int32, (8, 128), 1)
    i128 = lax.broadcasted_iota(jnp.int32, (128, 128), 0)
    j128 = lax.broadcasted_iota(jnp.int32, (128, 128), 1)
    wide = lambda v: jnp.broadcast_to(v, (1, 128))
    tile = lambda v: jnp.broadcast_to(v, (8, 128))
    here = slice(lo - top, hi - top)
    block = z_ref[here, lo:hi]
    part = [block[8 * g : 8 * g + 8] for g in range(16)]
    for q in range(0, 128, 2):
        gq, sq = q // 8, q % 8
        first, second = part[gq][sq : sq + 1, :], part[gq][sq + 1 : sq + 2, :]
        a, b, c = wide(first[:, q : q + 1]), wide(second[:, q : q + 1]), wide(second[:, q + 1 : q + 2])
        inverse = 1.0 / (a * c - b * b)
        l1 = lane[:1]
        one = jnp.where(l1 == q, c, jnp.where(l1 == q + 1, -b, c * first - b * second)) * inverse
        two = jnp.where(l1 == q, -b, jnp.where(l1 == q + 1, a, a * second - b * first)) * inverse
        one, two = tile(one), tile(two)
        pair = (lane == q) | (lane == q + 1)
        for g in range(gq, 16):
            if g == gq and sq == 6:
                continue
            left, right = tile(part[g][:, q : q + 1]), tile(part[g][:, q + 1 : q + 2])
            if g == gq:
                below = sub > sq + 1
                left, right = jnp.where(below, left, 0.0), jnp.where(below, right, 0.0)
                kept = jnp.where(pair & below, 0.0, part[g])
            else:
                kept = jnp.where(pair, 0.0, part[g])
            part[g] = (kept - left * one) - right * two
    done = jnp.concatenate(part, 0)
    odd = lax.rem(i128, 2) == 1
    diag = jnp.sum(jnp.where(i128 == j128, done, 0.0), axis=1, keepdims=True)
    beside = jnp.sum(jnp.where((j128 == i128 - 1) & odd, done, 0.0), axis=1, keepdims=True)
    unit = jnp.where(i128 == j128, 1.0, jnp.where(j128 < i128 - jnp.where(odd, 1, 0), done, 0.0))
    above = pltpu.roll(unit, 1, 0)
    ratio = jnp.where(odd[:, :1], beside / pltpu.roll(diag, 1, 0), 0.0)
    unit = unit - ratio * above
    pivots = diag - ratio * beside
    scale = lax.rsqrt(pivots)
    scale = scale * (1.5 - 0.5 * pivots * scale * scale)
    own = unit * scale
    x_ref[:, lo:hi] = own
    if lo:
        left = dot(own, z_ref[here, :lo])
        x_ref[:, :lo] = left
    if hi < PANEL:
        down = dot(z_ref[hi - top :, lo:hi], own, 1, 1)
        if lo:
            o_ref[:, :lo] = z_ref[hi - top :, :lo] - dot(down, left)
        o_ref[:, lo:hi] = -dot(down, own)
        o_ref[:, hi:] = z_ref[hi - top :, hi:] - dot(down, dot(own, z_ref[here, hi:]))


def factor_inverse(at, gram, mate):
    n = PANEL
    shape = lambda r, c: jax.ShapeDtypeStruct((r, c), jnp.float32)
    step = lambda kernel, out, ins, scratch, k: pl.pallas_call(
        kernel,
        out_shape=out,
        in_specs=ins,
        out_specs=[VMEM] * len(out),
        scratch_shapes=scratch,
        compiler_params=pltpu.CompilerParams(vmem_limit_bytes=LIMIT),
        cost_estimate=pl.CostEstimate(flops=k * 10**10, bytes_accessed=n * n * 4, transcendentals=0),
    )
    square = [pltpu.VMEM((n, n), jnp.float32)]
    l0, z = step(first_factor_kernel, [shape(128, 128), shape(384, n)], [SMEM, VMEM, VMEM], square, 1)(at, gram, mate)
    l1, z = step(second_factor_kernel, [shape(128, 256), shape(256, n)], [VMEM], [], 1)(z)
    rest = [pltpu.VMEM((128, n), jnp.float32)]
    l2, l3 = step(last_factor_kernel, [shape(128, 384), shape(128, n)], [VMEM], rest, 2)(z)
    return l0, l1, l2, l3


def assembled(at_ref, refs, g_ref):
    step = PANEL // X
    for s, ref in zip((0, 2, 1, 3), refs):
        row = pl.multiple_of(lax.rem(at_ref[0] + X - s, X) * step, step)
        g_ref[pl.ds(row, step), :] = ref[...]


def first_final_kernel(mid, at_ref, l0, l1, l2, l3, p_ref, m_ref, b0, b1, b2, b3, o_ref, r_ref, q_ref, g_ref):
    root = math.sqrt(X * Z * p_ref.shape[0])
    p = at_ref[2] * C + at_ref[3]
    q_ref[...] = jnp.concatenate([dot(p_ref[:, : l.shape[1]], l[...], 1, 1) for l in (l0, l1, l2, l3)], 1)
    assembled(at_ref, (b0, b1, b2, b3), g_ref)

    def columns(t, _):
        at = pl.ds(pl.multiple_of(t * 256, 256), 256)
        rows = jnp.concatenate([dot(l[...], g_ref[: l.shape[1], at]) for l in (l0, l1, l2, l3)], 0)
        r_ref[:, at] = rows * (1.0 / root)
        updated = m_ref[:, at] - dot(q_ref[...], rows)
        o_ref[:, at] = jnp.where(p == 0, q_ref[:, at] * root, updated)
        return 0

    lax.fori_loop(0, mid // 256, columns, 0)


def second_final_kernel(at_ref, l0, l1, l2, l3, q_ref, m_ref, b0, b1, b2, b3, o_in, r_in, o_ref, r_ref, g_ref):
    root = math.sqrt(X * Z * q_ref.shape[0])
    assembled(at_ref, (b0, b1, b2, b3), g_ref)

    def columns(t, _):
        at = pl.ds(pl.multiple_of(t * 256, 256), 256)
        rows = jnp.concatenate([dot(l[...], g_ref[: l.shape[1], at]) for l in (l0, l1, l2, l3)], 0)
        r_ref[:, at] = rows * (1.0 / root)
        o_ref[:, at] = m_ref[:, at] - dot(q_ref[...], rows)
        return 0

    lax.fori_loop(0, m_ref.shape[1] // 256, columns, 0)


def exchanged(blocks, axis):
    return lax.all_to_all(blocks, axis, 0, 0, tiled=False)


def everywhere(block, axis, size):
    return exchanged(jnp.broadcast_to(block[None], (size,) + block.shape), axis)


def shift(block, axis, size, by):
    return lax.ppermute(block, axis, [(i, (i + by) % size) for i in range(size)])


def local(initial_carry, forcing, transition, partials, arc_of_row, counts):
    f32 = jnp.float32
    x, z = lax.axis_index("x"), lax.axis_index("z")
    p = lax.axis_index(("y", "core"))
    width = initial_carry.shape[1]
    rows = partials.shape[1]
    blocks = transition.shape[0]
    core, y = lax.axis_index("core"), lax.axis_index("y")
    at = jnp.stack([x, z, y, core])
    maps = transition.transpose(0, 3, 1, 2).reshape(blocks, ARCS, STATE * STATE)
    maps = jnp.pad(maps, ((0, 0), (0, 0), (0, 128 - STATE * STATE)))

    packed = call(offsets_kernel, jax.ShapeDtypeStruct((Z, PACK, 128), f32), 2, (10**7, 10**6))(maps, forcing)
    received = exchanged(packed, "z")
    total = call(totals_kernel, jax.ShapeDtypeStruct((PACK, 128), f32), 1, (10**6, 10**5))(received)
    totals = [shift(total, "x", X, k) for k in range(1, X)]
    incoming = call(incoming_kernel, jax.ShapeDtypeStruct((Z, S, 128), f32), 6, (10**6, 10**5), (0,))(
        at, *totals, received, initial_carry
    )
    incoming = exchanged(incoming, "z")
    matrix, panel = pl.pallas_call(
        design_kernel,
        out_shape=[jax.ShapeDtypeStruct((rows, width), f32), jax.ShapeDtypeStruct((rows, PANEL), f32)],
        in_specs=[SMEM] + [VMEM] * 5,
        out_specs=[VMEM, VMEM],
        scratch_shapes=[pltpu.VMEM((blocks * S, width), f32)],
        compiler_params=pltpu.CompilerParams(vmem_limit_bytes=LIMIT),
        cost_estimate=pl.CostEstimate(flops=10**8, bytes_accessed=10**6, transcendentals=0),
    )(counts, incoming, maps, forcing, partials, arc_of_row[None, :])

    both = ("y", "core")
    right, far, left = [lax.ppermute(panel, both, [(0, k)]) for k in (2, 4, 6)]
    panel = jnp.where(p == 2, right, jnp.where(p == 4, far, jnp.where(p == 6, left, panel)))
    other = lax.ppermute(panel, both, [(0, 1), (2, 3), (4, 5), (6, 7)])
    panel = jnp.where(lax.axis_index("core") == 1, other, panel)

    half, quarter, step = PANEL // C, PANEL // Y, PANEL // X
    tile, mid = step // Z, PANEL
    gram = dot(
        lax.dynamic_slice(panel, (0, core * half), (rows, half)),
        lax.dynamic_slice(panel, (0, y * quarter), (rows, quarter)),
        0, 0,
    )
    gram, panel = lax.optimization_barrier((gram, panel))
    gram = exchanged(gram.reshape(X * Z, half // X // Z, quarter), ("x", "z"))
    gram = gram.sum(0)
    turned = lax.dynamic_slice(jnp.concatenate([panel, panel], 1), (0, x * step), (rows, PANEL))
    parts = [dot(turned[:, k * step : (k + 1) * step], matrix, 0, 0) for k in range(X)]
    sent = [shift(parts[k], "x", X, k) for k in (2, 1, 3)]
    gram = everywhere(gram, ("x", "z"), X * Z).reshape(half, quarter)
    gram, sent = lax.optimization_barrier((gram, sent))
    gram = [gram] + [shift(gram, "y", Y, k) for k in (1, 2, 3)]
    gram = jnp.stack(gram, 0)
    mate = lax.ppermute(gram, "core", [(0, 1), (1, 0)])

    products = parts[0] + sent[0] + sent[1] + sent[2]
    products = exchanged(products.reshape(Z, tile, width), "z")
    products = products.sum(0)
    products = everywhere(products, "z", Z).reshape(step, width)
    a = [products[:, :mid]]
    a += [shift(a[0], "x", X, k) for k in (2, 1, 3)]
    b = [products[:, mid:]]
    b += [shift(b[0], "x", X, k) for k in (2, 1, 3)]

    inverse = factor_inverse(at, gram, mate)
    half = jax.ShapeDtypeStruct((rows, width), f32), jax.ShapeDtypeStruct((PANEL, width), f32)
    packed, r_rows, basis = pl.pallas_call(
        functools.partial(first_final_kernel, mid),
        grid=(1,),
        out_shape=[*half, jax.ShapeDtypeStruct((rows, PANEL), f32)],
        in_specs=[SMEM] + [VMEM] * 10,
        out_specs=[pl.BlockSpec((rows, mid), lambda i: (0, 0)), pl.BlockSpec((PANEL, mid), lambda i: (0, 0)), VMEM],
        scratch_shapes=[pltpu.VMEM((PANEL, mid), f32)],
        compiler_params=pltpu.CompilerParams(vmem_limit_bytes=LIMIT),
        cost_estimate=pl.CostEstimate(flops=2 * 10**9, bytes_accessed=3 * 10**6, transcendentals=0),
    )(at, *inverse, panel, matrix[:, :mid], *a)
    return pl.pallas_call(
        second_final_kernel,
        grid=(1,),
        out_shape=half,
        in_specs=[SMEM] + [VMEM] * 10 + [pl.BlockSpec(memory_space=pl.ANY)] * 2,
        out_specs=[pl.BlockSpec((rows, width - mid), lambda i: (0, 1)), pl.BlockSpec((PANEL, width - mid), lambda i: (0, 1))],
        scratch_shapes=[pltpu.VMEM((PANEL, width - mid), f32)],
        input_output_aliases={11: 0, 12: 1},
        compiler_params=pltpu.CompilerParams(vmem_limit_bytes=LIMIT),
        cost_estimate=pl.CostEstimate(flops=2 * 10**9, bytes_accessed=3 * 10**6, transcendentals=0),
    )(at, *inverse, basis, matrix[:, mid:], *b, packed, r_rows)


def solution(mesh):
    mesh = Mesh(mesh.devices.reshape(X, Z, Y, C), ("x", "z", "y", "core"))
    e, q = ("x", "z"), ("y", "core")
    return jax.shard_map(
        local,
        mesh=mesh,
        in_specs=(P(None, q), P(e, None, q), P(e, None, None, None), P(None, e), P(e), P(e)),
        out_specs=(P(e, q), P(None, q)),
        check_vma=False,
    )
```

```python
import functools
import math

import jax
import jax.numpy as jnp
from jax import lax
from jax.experimental import pallas as pl
from jax.experimental.pallas import tpu as pltpu
from jax.sharding import Mesh
from jax.sharding import PartitionSpec as P


PANEL = 512
X, Z, Y, C = 4, 8, 4, 2
STATE, ARCS = 6, 8
S = STATE * ARCS
PACK = S + 8
LIMIT = 12 * 2**20
HI = lax.Precision.HIGHEST
VMEM = pl.BlockSpec(memory_space=pltpu.VMEM)
SMEM = pl.BlockSpec(memory_space=pltpu.SMEM)


def call(kernel, out, n, cost, smem=()):
    flops, size = cost
    return pl.pallas_call(
        kernel,
        out_shape=out,
        in_specs=[SMEM if i in smem else VMEM for i in range(n)],
        out_specs=VMEM if not isinstance(out, (tuple, list)) else [VMEM] * len(out),
        compiler_params=pltpu.CompilerParams(vmem_limit_bytes=LIMIT),
        cost_estimate=pl.CostEstimate(flops=flops, bytes_accessed=size, transcendentals=0),
    )


def dot(a, b, ca=1, cb=0):
    return lax.dot_general(a, b, (((ca,), (cb,)), ((), ())), precision=HI, preferred_element_type=jnp.float32)


def coefficients(tile):
    spread = lambda k: jnp.broadcast_to(tile[:, k : k + 1], (ARCS, 128))
    return [[spread(c * STATE + d) for d in range(STATE)] for c in range(STATE)]


def moved(coefficient, parts):
    out = []
    for row in coefficient:
        total = row[0] * parts[0]
        for d in range(1, STATE):
            total = total + row[d] * parts[d]
        out.append(total)
    return out


def split(value):
    return [value[c * ARCS : (c + 1) * ARCS] for c in range(STATE)]


def opened(tile):
    return [tile] + [pltpu.roll(tile, 128 - c * STATE, 1) for c in range(1, STATE)]


def closed(parts):
    lane = lax.broadcasted_iota(jnp.int32, (ARCS, 128), 1)
    parts = [jnp.where(lane < STATE, part, 0.0) for part in parts]
    out = parts[0]
    for c in range(1, STATE):
        out = out + pltpu.roll(parts[c], c * STATE, 1)
    return out


def offsets_kernel(d_ref, f_ref, o_ref):
    forced = lambda j, z: split(f_ref[j, :, z * 128 : (z + 1) * 128].astype(jnp.float32))
    whole = opened(d_ref[0])
    for j in range(1, d_ref.shape[0]):
        coefficient = coefficients(d_ref[j])
        for z in range(Z):
            parts = forced(0, z) if j == 1 else split(o_ref[z, :S, :])
            parts = moved(coefficient, parts)
            o_ref[z, :S, :] = jnp.concatenate([u + v for u, v in zip(parts, forced(j, z))], 0)
        whole = moved(coefficient, whole)
    whole = closed(whole)
    for z in range(Z):
        o_ref[z, S:, :] = whole


def totals_kernel(r_ref, o_ref):
    total = split(r_ref[0, :S, :])
    whole = opened(r_ref[0, S:, :])
    for z in range(1, Z):
        coefficient = coefficients(r_ref[z, S:, :])
        total = [u + v for u, v in zip(moved(coefficient, total), split(r_ref[z, :S, :]))]
        whole = moved(coefficient, whole)
    o_ref[:S, :] = jnp.concatenate(total, 0)
    o_ref[S:, :] = closed(whole)


def incoming_kernel(at_ref, t1, t2, t3, r_ref, i_ref, o_ref):
    x = at_ref[0]
    carry = split(i_ref[:, pl.ds(pl.multiple_of(at_ref[1] * 128, 128), 128)])
    for s, ref in ((3, t3), (2, t2), (1, t1)):
        after = moved(coefficients(ref[S:, :]), carry)
        carry = [jnp.where(s <= x, u + v, w) for u, v, w in zip(after, split(ref[:S, :]), carry)]
    for z in range(Z):
        o_ref[z] = jnp.concatenate(carry, 0)
        if z < Z - 1:
            after = moved(coefficients(r_ref[z, S:, :]), carry)
            carry = [u + v for u, v in zip(after, split(r_ref[z, :S, :]))]


def design_kernel(n_ref, i_ref, d_ref, f_ref, p_ref, a_ref, o_ref, h_ref, c_ref):
    blocks = d_ref.shape[0]
    rows = p_ref.shape[1]
    length = rows // blocks
    lane = lax.broadcasted_iota(jnp.int32, (ARCS, rows), 1)
    arc = lax.broadcasted_iota(jnp.int32, (ARCS, rows), 0)
    chosen = arc == a_ref[...]
    weights = []
    for j in range(blocks):
        live = (lane >= j * length) & (lane < j * length + jnp.minimum(n_ref[j], length)) & chosen
        for c in range(STATE):
            weights.append(jnp.where(live, p_ref[c : c + 1, :], 0.0))
    weights = jnp.concatenate(weights, 0)
    for j in range(blocks):
        coefficient = coefficients(d_ref[j])
        for z in range(Z):
            at = slice(z * 128, (z + 1) * 128)
            before = i_ref[z] if j == 0 else c_ref[(j - 1) * S : j * S, at]
            parts = zip(moved(coefficient, split(before)), split(f_ref[j, :, at].astype(jnp.float32)))
            c_ref[j * S : (j + 1) * S, at] = jnp.concatenate([u + v for u, v in parts], 0)
    out = dot(weights, c_ref[...], 0, 0)
    o_ref[...] = out
    h_ref[...] = out[:, :PANEL]


def first_factor_kernel(at_ref, g_ref, m_ref, x_ref, o_ref, z_ref):
    n = z_ref.shape[0]
    half = n // C
    for c in range(C):
        source = m_ref if c else g_ref
        row = pl.multiple_of(lax.rem(at_ref[3] + c, C) * half, half)
        for u in range(Y):
            column = pl.multiple_of(lax.rem(at_ref[2] + Y - u, Y) * 128, 128)
            z_ref[pl.ds(row, half), pl.ds(column, 128)] = source[u]
    factor_block(0, x_ref, z_ref, 0, o_ref)


def second_factor_kernel(z_ref, x_ref, o_ref):
    factor_block(1, x_ref, z_ref, 128, o_ref)


def third_factor_kernel(z_ref, x_ref, o_ref):
    factor_block(2, x_ref, z_ref, 256, o_ref)


def last_factor_kernel(z_ref, x_ref):
    factor_block(3, x_ref, z_ref, 384, None)


def factor_block(k, x_ref, z_ref, top, o_ref):
    lo, hi = k * 128, k * 128 + 128
    sub = lax.broadcasted_iota(jnp.int32, (8, 128), 0)
    lane = lax.broadcasted_iota(jnp.int32, (8, 128), 1)
    i128 = lax.broadcasted_iota(jnp.int32, (128, 128), 0)
    j128 = lax.broadcasted_iota(jnp.int32, (128, 128), 1)
    wide = lambda v: jnp.broadcast_to(v, (1, 128))
    tile = lambda v: jnp.broadcast_to(v, (8, 128))
    here = slice(lo - top, hi - top)
    block = z_ref[here, lo:hi]
    part = [block[8 * g : 8 * g + 8] for g in range(16)]
    for q in range(0, 128, 2):
        gq, sq = q // 8, q % 8
        first, second = part[gq][sq : sq + 1, :], part[gq][sq + 1 : sq + 2, :]
        a, b, c = wide(first[:, q : q + 1]), wide(second[:, q : q + 1]), wide(second[:, q + 1 : q + 2])
        inverse = 1.0 / (a * c - b * b)
        l1 = lane[:1]
        one = jnp.where(l1 == q, c, jnp.where(l1 == q + 1, -b, c * first - b * second)) * inverse
        two = jnp.where(l1 == q, -b, jnp.where(l1 == q + 1, a, a * second - b * first)) * inverse
        one, two = tile(one), tile(two)
        pair = (lane == q) | (lane == q + 1)
        for g in range(gq, 16):
            if g == gq and sq == 6:
                continue
            left, right = tile(part[g][:, q : q + 1]), tile(part[g][:, q + 1 : q + 2])
            if g == gq:
                below = sub > sq + 1
                left, right = jnp.where(below, left, 0.0), jnp.where(below, right, 0.0)
                kept = jnp.where(pair & below, 0.0, part[g])
            else:
                kept = jnp.where(pair, 0.0, part[g])
            part[g] = (kept - left * one) - right * two
    done = jnp.concatenate(part, 0)
    odd = lax.rem(i128, 2) == 1
    diag = jnp.sum(jnp.where(i128 == j128, done, 0.0), axis=1, keepdims=True)
    beside = jnp.sum(jnp.where((j128 == i128 - 1) & odd, done, 0.0), axis=1, keepdims=True)
    unit = jnp.where(i128 == j128, 1.0, jnp.where(j128 < i128 - jnp.where(odd, 1, 0), done, 0.0))
    above = pltpu.roll(unit, 1, 0)
    ratio = jnp.where(odd[:, :1], beside / pltpu.roll(diag, 1, 0), 0.0)
    unit = unit - ratio * above
    pivots = diag - ratio * beside
    scale = lax.rsqrt(pivots)
    scale = scale * (1.5 - 0.5 * pivots * scale * scale)
    own = unit * scale
    x_ref[:, lo:hi] = own
    if lo:
        left = dot(own, z_ref[here, :lo])
        x_ref[:, :lo] = left
    if hi < PANEL:
        down = dot(z_ref[hi - top :, lo:hi], own, 1, 1)
        if lo:
            o_ref[:, :lo] = z_ref[hi - top :, :lo] - dot(down, left)
        o_ref[:, lo:hi] = -dot(down, own)
        o_ref[:, hi:] = z_ref[hi - top :, hi:] - dot(down, dot(own, z_ref[here, hi:]))


def factor_inverse(at, gram, mate):
    n = PANEL
    shape = lambda r, c: jax.ShapeDtypeStruct((r, c), jnp.float32)
    step = lambda kernel, out, ins, scratch, k: pl.pallas_call(
        kernel,
        out_shape=out,
        in_specs=ins,
        out_specs=[VMEM] * len(out),
        scratch_shapes=scratch,
        compiler_params=pltpu.CompilerParams(vmem_limit_bytes=LIMIT),
        cost_estimate=pl.CostEstimate(flops=k * 10**10, bytes_accessed=n * n * 4, transcendentals=0),
    )
    square = [pltpu.VMEM((n, n), jnp.float32)]
    l0, z = step(first_factor_kernel, [shape(128, 128), shape(384, n)], [SMEM, VMEM, VMEM], square, 1)(at, gram, mate)
    l1, z = step(second_factor_kernel, [shape(128, 256), shape(256, n)], [VMEM], [], 1)(z)
    l2, z = step(third_factor_kernel, [shape(128, 384), shape(128, n)], [VMEM], [], 1)(z)
    (l3,) = step(last_factor_kernel, [shape(128, n)], [VMEM], [], 1)(z)
    return l0, l1, l2, l3


def assembled(at_ref, refs, g_ref):
    step = PANEL // X
    for s, ref in zip((0, 2, 1, 3), refs):
        row = pl.multiple_of(lax.rem(at_ref[0] + X - s, X) * step, step)
        g_ref[pl.ds(row, step), :] = ref[...]


def first_final_kernel(mid, at_ref, l0, l1, l2, l3, p_ref, m_ref, b0, b1, b2, b3, o_ref, r_ref, q_ref, g_ref):
    root = math.sqrt(X * Z * p_ref.shape[0])
    p = at_ref[2] * C + at_ref[3]
    q_ref[...] = jnp.concatenate([dot(p_ref[:, : l.shape[1]], l[...], 1, 1) for l in (l0, l1, l2, l3)], 1)
    assembled(at_ref, (b0, b1, b2, b3), g_ref)

    def columns(t, _):
        at = pl.ds(pl.multiple_of(t * 256, 256), 256)
        rows = jnp.concatenate([dot(l[...], g_ref[: l.shape[1], at]) for l in (l0, l1, l2, l3)], 0)
        r_ref[:, at] = rows * (1.0 / root)
        updated = m_ref[:, at] - dot(q_ref[...], rows)
        o_ref[:, at] = jnp.where(p == 0, q_ref[:, at] * root, updated)
        return 0

    lax.fori_loop(0, mid // 256, columns, 0)


def second_final_kernel(at_ref, l0, l1, l2, l3, q_ref, m_ref, b0, b1, b2, b3, o_in, r_in, o_ref, r_ref, g_ref):
    root = math.sqrt(X * Z * q_ref.shape[0])
    assembled(at_ref, (b0, b1, b2, b3), g_ref)

    def columns(t, _):
        at = pl.ds(pl.multiple_of(t * 256, 256), 256)
        rows = jnp.concatenate([dot(l[...], g_ref[: l.shape[1], at]) for l in (l0, l1, l2, l3)], 0)
        r_ref[:, at] = rows * (1.0 / root)
        o_ref[:, at] = m_ref[:, at] - dot(q_ref[...], rows)
        return 0

    lax.fori_loop(0, m_ref.shape[1] // 256, columns, 0)


def exchanged(blocks, axis):
    return lax.all_to_all(blocks, axis, 0, 0, tiled=False)


def everywhere(block, axis, size):
    return exchanged(jnp.broadcast_to(block[None], (size,) + block.shape), axis)


def shift(block, axis, size, by):
    return lax.ppermute(block, axis, [(i, (i + by) % size) for i in range(size)])


def local(initial_carry, forcing, transition, partials, arc_of_row, counts):
    f32 = jnp.float32
    x, z = lax.axis_index("x"), lax.axis_index("z")
    p = lax.axis_index(("y", "core"))
    width = initial_carry.shape[1]
    rows = partials.shape[1]
    blocks = transition.shape[0]
    core, y = lax.axis_index("core"), lax.axis_index("y")
    at = jnp.stack([x, z, y, core])
    maps = transition.transpose(0, 3, 1, 2).reshape(blocks, ARCS, STATE * STATE)
    maps = jnp.pad(maps, ((0, 0), (0, 0), (0, 128 - STATE * STATE)))

    packed = call(offsets_kernel, jax.ShapeDtypeStruct((Z, PACK, 128), f32), 2, (10**7, 10**6))(maps, forcing)
    received = exchanged(packed, "z")
    total = call(totals_kernel, jax.ShapeDtypeStruct((PACK, 128), f32), 1, (10**6, 10**5))(received)
    totals = [shift(total, "x", X, k) for k in range(1, X)]
    incoming = call(incoming_kernel, jax.ShapeDtypeStruct((Z, S, 128), f32), 6, (10**6, 10**5), (0,))(
        at, *totals, received, initial_carry
    )
    incoming = exchanged(incoming, "z")
    matrix, panel = pl.pallas_call(
        design_kernel,
        out_shape=[jax.ShapeDtypeStruct((rows, width), f32), jax.ShapeDtypeStruct((rows, PANEL), f32)],
        in_specs=[SMEM] + [VMEM] * 5,
        out_specs=[VMEM, VMEM],
        scratch_shapes=[pltpu.VMEM((blocks * S, width), f32)],
        compiler_params=pltpu.CompilerParams(vmem_limit_bytes=LIMIT),
        cost_estimate=pl.CostEstimate(flops=10**8, bytes_accessed=10**6, transcendentals=0),
    )(counts, incoming, maps, forcing, partials, arc_of_row[None, :])

    both = ("y", "core")
    right, far, left = [lax.ppermute(panel, both, [(0, k)]) for k in (2, 4, 6)]
    panel = jnp.where(p == 2, right, jnp.where(p == 4, far, jnp.where(p == 6, left, panel)))
    other = lax.ppermute(panel, both, [(0, 1), (2, 3), (4, 5), (6, 7)])
    panel = jnp.where(lax.axis_index("core") == 1, other, panel)

    half, quarter, step = PANEL // C, PANEL // Y, PANEL // X
    tile, mid = step // Z, PANEL
    gram = dot(
        lax.dynamic_slice(panel, (0, core * half), (rows, half)),
        lax.dynamic_slice(panel, (0, y * quarter), (rows, quarter)),
        0, 0,
    )
    gram, panel = lax.optimization_barrier((gram, panel))
    gram = exchanged(gram.reshape(X * Z, half // X // Z, quarter), ("x", "z"))
    gram = gram.sum(0)
    turned = lax.dynamic_slice(jnp.concatenate([panel, panel], 1), (0, x * step), (rows, PANEL))
    parts = [dot(turned[:, k * step : (k + 1) * step], matrix, 0, 0) for k in range(X)]
    sent = [shift(parts[k], "x", X, k) for k in (2, 1, 3)]
    gram = everywhere(gram, ("x", "z"), X * Z).reshape(half, quarter)
    gram, sent = lax.optimization_barrier((gram, sent))
    gram = [gram] + [shift(gram, "y", Y, k) for k in (1, 2, 3)]
    gram = jnp.stack(gram, 0)
    mate = lax.ppermute(gram, "core", [(0, 1), (1, 0)])

    products = parts[0] + sent[0] + sent[1] + sent[2]
    products = exchanged(products.reshape(Z, tile, width), "z")
    products = products.sum(0)
    products = everywhere(products, "z", Z)
    products = products.reshape(step, width)
    a = [products[:, :mid]]
    a += [shift(a[0], "x", X, k) for k in (2, 1, 3)]
    b = [products[:, mid:]]
    b += [shift(b[0], "x", X, k) for k in (2, 1, 3)]

    inverse = factor_inverse(at, gram, mate)
    half = jax.ShapeDtypeStruct((rows, width), f32), jax.ShapeDtypeStruct((PANEL, width), f32)
    packed, r_rows, basis = pl.pallas_call(
        functools.partial(first_final_kernel, mid),
        grid=(1,),
        out_shape=[*half, jax.ShapeDtypeStruct((rows, PANEL), f32)],
        in_specs=[SMEM] + [VMEM] * 10,
        out_specs=[pl.BlockSpec((rows, mid), lambda i: (0, 0)), pl.BlockSpec((PANEL, mid), lambda i: (0, 0)), VMEM],
        scratch_shapes=[pltpu.VMEM((PANEL, mid), f32)],
        compiler_params=pltpu.CompilerParams(vmem_limit_bytes=LIMIT),
        cost_estimate=pl.CostEstimate(flops=2 * 10**9, bytes_accessed=3 * 10**6, transcendentals=0),
    )(at, *inverse, panel, matrix[:, :mid], *a)
    return pl.pallas_call(
        second_final_kernel,
        grid=(1,),
        out_shape=half,
        in_specs=[SMEM] + [VMEM] * 10 + [pl.BlockSpec(memory_space=pl.ANY)] * 2,
        out_specs=[pl.BlockSpec((rows, width - mid), lambda i: (0, 1)), pl.BlockSpec((PANEL, width - mid), lambda i: (0, 1))],
        scratch_shapes=[pltpu.VMEM((PANEL, width - mid), f32)],
        input_output_aliases={11: 0, 12: 1},
        compiler_params=pltpu.CompilerParams(vmem_limit_bytes=LIMIT),
        cost_estimate=pl.CostEstimate(flops=2 * 10**9, bytes_accessed=3 * 10**6, transcendentals=0),
    )(at, *inverse, basis, matrix[:, mid:], *b, packed, r_rows)


def solution(mesh):
    mesh = Mesh(mesh.devices.reshape(X, Z, Y, C), ("x", "z", "y", "core"))
    e, q = ("x", "z"), ("y", "core")
    return jax.shard_map(
        local,
        mesh=mesh,
        in_specs=(P(None, q), P(e, None, q), P(e, None, None, None), P(None, e), P(e), P(e)),
        out_specs=(P(e, q), P(None, q)),
        check_vma=False,
    )
```

```python
import functools
import math

import jax
import jax.numpy as jnp
from jax import lax
from jax.experimental import pallas as pl
from jax.experimental.pallas import tpu as pltpu
from jax.sharding import Mesh
from jax.sharding import PartitionSpec as P


PANEL = 512
X, Z, Y, C = 4, 8, 4, 2
STATE, ARCS = 6, 8
S = STATE * ARCS
PACK = S + 8
LIMIT = 12 * 2**20
HI = lax.Precision.HIGHEST
VMEM = pl.BlockSpec(memory_space=pltpu.VMEM)
SMEM = pl.BlockSpec(memory_space=pltpu.SMEM)


def call(kernel, out, n, cost, smem=()):
    flops, size = cost
    return pl.pallas_call(
        kernel,
        out_shape=out,
        in_specs=[SMEM if i in smem else VMEM for i in range(n)],
        out_specs=VMEM if not isinstance(out, (tuple, list)) else [VMEM] * len(out),
        compiler_params=pltpu.CompilerParams(vmem_limit_bytes=LIMIT),
        cost_estimate=pl.CostEstimate(flops=flops, bytes_accessed=size, transcendentals=0),
    )


def dot(a, b, ca=1, cb=0):
    return lax.dot_general(a, b, (((ca,), (cb,)), ((), ())), precision=HI, preferred_element_type=jnp.float32)


def coefficients(tile):
    spread = lambda k: jnp.broadcast_to(tile[:, k : k + 1], (ARCS, 128))
    return [[spread(c * STATE + d) for d in range(STATE)] for c in range(STATE)]


def moved(coefficient, parts):
    out = []
    for row in coefficient:
        total = row[0] * parts[0]
        for d in range(1, STATE):
            total = total + row[d] * parts[d]
        out.append(total)
    return out


def split(value):
    return [value[c * ARCS : (c + 1) * ARCS] for c in range(STATE)]


def opened(tile):
    return [tile] + [pltpu.roll(tile, 128 - c * STATE, 1) for c in range(1, STATE)]


def closed(parts):
    lane = lax.broadcasted_iota(jnp.int32, (ARCS, 128), 1)
    parts = [jnp.where(lane < STATE, part, 0.0) for part in parts]
    out = parts[0]
    for c in range(1, STATE):
        out = out + pltpu.roll(parts[c], c * STATE, 1)
    return out


def offsets_kernel(d_ref, f_ref, o_ref):
    forced = lambda j, z: split(f_ref[j, :, z * 128 : (z + 1) * 128].astype(jnp.float32))
    whole = opened(d_ref[0])
    for j in range(1, d_ref.shape[0]):
        coefficient = coefficients(d_ref[j])
        for z in range(Z):
            parts = forced(0, z) if j == 1 else split(o_ref[z, :S, :])
            parts = moved(coefficient, parts)
            o_ref[z, :S, :] = jnp.concatenate([u + v for u, v in zip(parts, forced(j, z))], 0)
        whole = moved(coefficient, whole)
    whole = closed(whole)
    for z in range(Z):
        o_ref[z, S:, :] = whole


def totals_kernel(r_ref, o_ref):
    total = split(r_ref[0, :S, :])
    whole = opened(r_ref[0, S:, :])
    for z in range(1, Z):
        coefficient = coefficients(r_ref[z, S:, :])
        total = [u + v for u, v in zip(moved(coefficient, total), split(r_ref[z, :S, :]))]
        whole = moved(coefficient, whole)
    o_ref[:S, :] = jnp.concatenate(total, 0)
    o_ref[S:, :] = closed(whole)


def incoming_kernel(at_ref, t1, t2, t3, r_ref, i_ref, o_ref):
    x = at_ref[0]
    carry = split(i_ref[:, pl.ds(pl.multiple_of(at_ref[1] * 128, 128), 128)])
    for s, ref in ((3, t3), (2, t2), (1, t1)):
        after = moved(coefficients(ref[S:, :]), carry)
        carry = [jnp.where(s <= x, u + v, w) for u, v, w in zip(after, split(ref[:S, :]), carry)]
    for z in range(Z):
        o_ref[z] = jnp.concatenate(carry, 0)
        if z < Z - 1:
            after = moved(coefficients(r_ref[z, S:, :]), carry)
            carry = [u + v for u, v in zip(after, split(r_ref[z, :S, :]))]


def design_kernel(n_ref, i_ref, d_ref, f_ref, p_ref, a_ref, o_ref, h_ref, c_ref):
    blocks = d_ref.shape[0]
    rows = p_ref.shape[1]
    length = rows // blocks
    lane = lax.broadcasted_iota(jnp.int32, (ARCS, rows), 1)
    arc = lax.broadcasted_iota(jnp.int32, (ARCS, rows), 0)
    chosen = arc == a_ref[...]
    weights = []
    for j in range(blocks):
        live = (lane >= j * length) & (lane < j * length + jnp.minimum(n_ref[j], length)) & chosen
        for c in range(STATE):
            weights.append(jnp.where(live, p_ref[c : c + 1, :], 0.0))
    weights = jnp.concatenate(weights, 0)
    for j in range(blocks):
        coefficient = coefficients(d_ref[j])
        for z in range(Z):
            at = slice(z * 128, (z + 1) * 128)
            before = i_ref[z] if j == 0 else c_ref[(j - 1) * S : j * S, at]
            parts = zip(moved(coefficient, split(before)), split(f_ref[j, :, at].astype(jnp.float32)))
            c_ref[j * S : (j + 1) * S, at] = jnp.concatenate([u + v for u, v in parts], 0)
    out = dot(weights, c_ref[...], 0, 0)
    o_ref[...] = out
    h_ref[...] = out[:, :PANEL]


def first_factor_kernel(at_ref, g_ref, m_ref, x_ref, o_ref, z_ref):
    n = z_ref.shape[0]
    half = n // C
    for c in range(C):
        source = m_ref if c else g_ref
        row = pl.multiple_of(lax.rem(at_ref[3] + c, C) * half, half)
        for u in range(Y):
            column = pl.multiple_of(lax.rem(at_ref[2] + Y - u, Y) * 128, 128)
            z_ref[pl.ds(row, half), pl.ds(column, 128)] = source[u]
    factor_block(0, x_ref, z_ref, 0, o_ref)


def second_factor_kernel(z_ref, x_ref, o_ref):
    factor_block(1, x_ref, z_ref, 128, o_ref)


def third_factor_kernel(z_ref, x_ref, o_ref):
    factor_block(2, x_ref, z_ref, 256, o_ref)


def last_factor_kernel(z_ref, x_ref):
    factor_block(3, x_ref, z_ref, 384, None)


def factor_block(k, x_ref, z_ref, top, o_ref):
    lo, hi = k * 128, k * 128 + 128
    sub = lax.broadcasted_iota(jnp.int32, (8, 128), 0)
    lane = lax.broadcasted_iota(jnp.int32, (8, 128), 1)
    i128 = lax.broadcasted_iota(jnp.int32, (128, 128), 0)
    j128 = lax.broadcasted_iota(jnp.int32, (128, 128), 1)
    wide = lambda v: jnp.broadcast_to(v, (1, 128))
    tile = lambda v: jnp.broadcast_to(v, (8, 128))
    here = slice(lo - top, hi - top)
    block = z_ref[here, lo:hi]
    part = [block[8 * g : 8 * g + 8] for g in range(16)]
    for q in range(0, 128, 2):
        gq, sq = q // 8, q % 8
        first, second = part[gq][sq : sq + 1, :], part[gq][sq + 1 : sq + 2, :]
        a, b, c = wide(first[:, q : q + 1]), wide(second[:, q : q + 1]), wide(second[:, q + 1 : q + 2])
        inverse = 1.0 / (a * c - b * b)
        l1 = lane[:1]
        one = jnp.where(l1 == q, c, jnp.where(l1 == q + 1, -b, c * first - b * second)) * inverse
        two = jnp.where(l1 == q, -b, jnp.where(l1 == q + 1, a, a * second - b * first)) * inverse
        one, two = tile(one), tile(two)
        pair = (lane == q) | (lane == q + 1)
        for g in range(gq, 16):
            if g == gq and sq == 6:
                continue
            left, right = tile(part[g][:, q : q + 1]), tile(part[g][:, q + 1 : q + 2])
            if g == gq:
                below = sub > sq + 1
                left, right = jnp.where(below, left, 0.0), jnp.where(below, right, 0.0)
                kept = jnp.where(pair & below, 0.0, part[g])
            else:
                kept = jnp.where(pair, 0.0, part[g])
            part[g] = (kept - left * one) - right * two
    done = jnp.concatenate(part, 0)
    odd = lax.rem(i128, 2) == 1
    diag = jnp.sum(jnp.where(i128 == j128, done, 0.0), axis=1, keepdims=True)
    beside = jnp.sum(jnp.where((j128 == i128 - 1) & odd, done, 0.0), axis=1, keepdims=True)
    unit = jnp.where(i128 == j128, 1.0, jnp.where(j128 < i128 - jnp.where(odd, 1, 0), done, 0.0))
    above = pltpu.roll(unit, 1, 0)
    ratio = jnp.where(odd[:, :1], beside / pltpu.roll(diag, 1, 0), 0.0)
    unit = unit - ratio * above
    pivots = diag - ratio * beside
    scale = lax.rsqrt(pivots)
    scale = scale * (1.5 - 0.5 * pivots * scale * scale)
    own = unit * scale
    x_ref[:, lo:hi] = own
    if lo:
        left = dot(own, z_ref[here, :lo])
        x_ref[:, :lo] = left
    if hi < PANEL:
        down = dot(z_ref[hi - top :, lo:hi], own, 1, 1)
        if lo:
            o_ref[:, :lo] = z_ref[hi - top :, :lo] - dot(down, left)
        o_ref[:, lo:hi] = -dot(down, own)
        o_ref[:, hi:] = z_ref[hi - top :, hi:] - dot(down, dot(own, z_ref[here, hi:]))


def factor_inverse(at, gram, mate):
    n = PANEL
    shape = lambda r, c: jax.ShapeDtypeStruct((r, c), jnp.float32)
    step = lambda kernel, out, ins, scratch, k: pl.pallas_call(
        kernel,
        out_shape=out,
        in_specs=ins,
        out_specs=[VMEM] * len(out),
        scratch_shapes=scratch,
        compiler_params=pltpu.CompilerParams(vmem_limit_bytes=LIMIT),
        cost_estimate=pl.CostEstimate(flops=k * 10**10, bytes_accessed=n * n * 4, transcendentals=0),
    )
    square = [pltpu.VMEM((n, n), jnp.float32)]
    l0, z = step(first_factor_kernel, [shape(128, 128), shape(384, n)], [SMEM, VMEM, VMEM], square, 1)(at, gram, mate)
    l1, z = step(second_factor_kernel, [shape(128, 256), shape(256, n)], [VMEM], [], 1)(z)
    l2, z = step(third_factor_kernel, [shape(128, 384), shape(128, n)], [VMEM], [], 1)(z)
    (l3,) = step(last_factor_kernel, [shape(128, n)], [VMEM], [], 1)(z)
    return l0, l1, l2, l3


def assembled(at_ref, refs, g_ref):
    step = PANEL // X
    for s, ref in zip((0, 2, 1, 3), refs):
        row = pl.multiple_of(lax.rem(at_ref[0] + X - s, X) * step, step)
        g_ref[pl.ds(row, step), :] = ref[...]


def first_final_kernel(mid, at_ref, l0, l1, l2, l3, p_ref, m_ref, b0, b1, b2, b3, o_ref, r_ref, q_ref, g_ref):
    root = math.sqrt(X * Z * p_ref.shape[0])
    p = at_ref[2] * C + at_ref[3]
    q_ref[...] = jnp.concatenate([dot(p_ref[:, : l.shape[1]], l[...], 1, 1) for l in (l0, l1, l2, l3)], 1)
    assembled(at_ref, (b0, b1, b2, b3), g_ref)

    def columns(t, _):
        at = pl.ds(pl.multiple_of(t * 256, 256), 256)
        rows = jnp.concatenate([dot(l[...], g_ref[: l.shape[1], at]) for l in (l0, l1, l2, l3)], 0)
        r_ref[:, at] = rows * (1.0 / root)
        updated = m_ref[:, at] - dot(q_ref[...], rows)
        o_ref[:, at] = jnp.where(p == 0, q_ref[:, at] * root, updated)
        return 0

    lax.fori_loop(0, mid // 256, columns, 0)


def second_final_kernel(at_ref, l0, l1, l2, l3, q_ref, m_ref, b0, b1, b2, b3, o_in, r_in, o_ref, r_ref, g_ref):
    root = math.sqrt(X * Z * q_ref.shape[0])
    assembled(at_ref, (b0, b1, b2, b3), g_ref)

    def columns(t, _):
        at = pl.ds(pl.multiple_of(t * 256, 256), 256)
        rows = jnp.concatenate([dot(l[...], g_ref[: l.shape[1], at]) for l in (l0, l1, l2, l3)], 0)
        r_ref[:, at] = rows * (1.0 / root)
        o_ref[:, at] = m_ref[:, at] - dot(q_ref[...], rows)
        return 0

    lax.fori_loop(0, m_ref.shape[1] // 256, columns, 0)


def exchanged(blocks, axis):
    return lax.all_to_all(blocks, axis, 0, 0, tiled=False)


def everywhere(block, axis, size):
    return exchanged(jnp.broadcast_to(block[None], (size,) + block.shape), axis)


def shift(block, axis, size, by):
    return lax.ppermute(block, axis, [(i, (i + by) % size) for i in range(size)])


def local(initial_carry, forcing, transition, partials, arc_of_row, counts):
    f32 = jnp.float32
    x, z = lax.axis_index("x"), lax.axis_index("z")
    p = lax.axis_index(("y", "core"))
    width = initial_carry.shape[1]
    rows = partials.shape[1]
    blocks = transition.shape[0]
    core, y = lax.axis_index("core"), lax.axis_index("y")
    at = jnp.stack([x, z, y, core])
    maps = transition.transpose(0, 3, 1, 2).reshape(blocks, ARCS, STATE * STATE)
    maps = jnp.pad(maps, ((0, 0), (0, 0), (0, 128 - STATE * STATE)))

    packed = call(offsets_kernel, jax.ShapeDtypeStruct((Z, PACK, 128), f32), 2, (10**7, 10**6))(maps, forcing)
    received = exchanged(packed, "z")
    total = call(totals_kernel, jax.ShapeDtypeStruct((PACK, 128), f32), 1, (10**6, 10**5))(received)
    totals = [shift(total, "x", X, k) for k in range(1, X)]
    incoming = call(incoming_kernel, jax.ShapeDtypeStruct((Z, S, 128), f32), 6, (10**6, 10**5), (0,))(
        at, *totals, received, initial_carry
    )
    incoming = exchanged(incoming, "z")
    matrix, panel = pl.pallas_call(
        design_kernel,
        out_shape=[jax.ShapeDtypeStruct((rows, width), f32), jax.ShapeDtypeStruct((rows, PANEL), f32)],
        in_specs=[SMEM] + [VMEM] * 5,
        out_specs=[VMEM, VMEM],
        scratch_shapes=[pltpu.VMEM((blocks * S, width), f32)],
        compiler_params=pltpu.CompilerParams(vmem_limit_bytes=LIMIT),
        cost_estimate=pl.CostEstimate(flops=10**8, bytes_accessed=10**6, transcendentals=0),
    )(counts, incoming, maps, forcing, partials, arc_of_row[None, :])

    both = ("y", "core")
    right, far, left = [lax.ppermute(panel, both, [(0, k)]) for k in (2, 4, 6)]
    panel = jnp.where(p == 2, right, jnp.where(p == 4, far, jnp.where(p == 6, left, panel)))
    other = lax.ppermute(panel, both, [(0, 1), (2, 3), (4, 5), (6, 7)])
    panel = jnp.where(lax.axis_index("core") == 1, other, panel)

    half, quarter, step = PANEL // C, PANEL // Y, PANEL // X
    tile, mid = step // Z, PANEL
    gram = dot(
        lax.dynamic_slice(panel, (0, core * half), (rows, half)),
        lax.dynamic_slice(panel, (0, y * quarter), (rows, quarter)),
        0, 0,
    )
    gram, panel = lax.optimization_barrier((gram, panel))
    gram = exchanged(gram.reshape(X * Z, half // X // Z, quarter), ("x", "z"))
    gram = gram.sum(0)
    turned = lax.dynamic_slice(jnp.concatenate([panel, panel], 1), (0, x * step), (rows, PANEL))
    tall = [turned[:, k * step : (k + 1) * step] for k in range(X)]
    parts = [[dot(t, m, 0, 0) for t in tall] for m in (matrix[:, :mid], matrix[:, mid:])]
    sent = [shift(parts[0][k], "x", X, k) for k in (2, 1, 3)]
    late = [shift(parts[1][k], "x", X, k) for k in (2, 1, 3)]

    gram = everywhere(gram, ("x", "z"), X * Z)
    gram = gram.reshape(half, quarter)
    gram = [gram] + [shift(gram, "y", Y, k) for k in (1, 2, 3)]
    gram = jnp.stack(gram, 0)
    gram, sent, late = lax.optimization_barrier((gram, sent, late))
    mate = lax.ppermute(gram, "core", [(0, 1), (1, 0)])

    products = [own[0] + got[0] + got[1] + got[2] for own, got in zip(parts, (sent, late))]
    products = jnp.concatenate(products, 1)
    products = exchanged(products.reshape(Z, tile, width), "z")
    products = products.sum(0)
    products = everywhere(products, "z", Z)
    products = products.reshape(step, width)
    a = [products[:, :mid]]
    a += [shift(a[0], "x", X, k) for k in (2, 1, 3)]
    b = [products[:, mid:]]
    b += [shift(b[0], "x", X, k) for k in (2, 1, 3)]

    inverse = factor_inverse(at, gram, mate)
    half = jax.ShapeDtypeStruct((rows, width), f32), jax.ShapeDtypeStruct((PANEL, width), f32)
    packed, r_rows, basis = pl.pallas_call(
        functools.partial(first_final_kernel, mid),
        grid=(1,),
        out_shape=[*half, jax.ShapeDtypeStruct((rows, PANEL), f32)],
        in_specs=[SMEM] + [VMEM] * 10,
        out_specs=[pl.BlockSpec((rows, mid), lambda i: (0, 0)), pl.BlockSpec((PANEL, mid), lambda i: (0, 0)), VMEM],
        scratch_shapes=[pltpu.VMEM((PANEL, mid), f32)],
        compiler_params=pltpu.CompilerParams(vmem_limit_bytes=LIMIT),
        cost_estimate=pl.CostEstimate(flops=2 * 10**9, bytes_accessed=3 * 10**6, transcendentals=0),
    )(at, *inverse, panel, matrix[:, :mid], *a)
    return pl.pallas_call(
        second_final_kernel,
        grid=(1,),
        out_shape=half,
        in_specs=[SMEM] + [VMEM] * 10 + [pl.BlockSpec(memory_space=pl.ANY)] * 2,
        out_specs=[pl.BlockSpec((rows, width - mid), lambda i: (0, 1)), pl.BlockSpec((PANEL, width - mid), lambda i: (0, 1))],
        scratch_shapes=[pltpu.VMEM((PANEL, width - mid), f32)],
        input_output_aliases={11: 0, 12: 1},
        compiler_params=pltpu.CompilerParams(vmem_limit_bytes=LIMIT),
        cost_estimate=pl.CostEstimate(flops=2 * 10**9, bytes_accessed=3 * 10**6, transcendentals=0),
    )(at, *inverse, basis, matrix[:, mid:], *b, packed, r_rows)


def solution(mesh):
    mesh = Mesh(mesh.devices.reshape(X, Z, Y, C), ("x", "z", "y", "core"))
    e, q = ("x", "z"), ("y", "core")
    return jax.shard_map(
        local,
        mesh=mesh,
        in_specs=(P(None, q), P(e, None, q), P(e, None, None, None), P(None, e), P(e), P(e)),
        out_specs=(P(e, q), P(None, q)),
        check_vma=False,
    )
```

```python
import functools
import math

import jax
import jax.numpy as jnp
from jax import lax
from jax.experimental import pallas as pl
from jax.experimental.pallas import tpu as pltpu
from jax.sharding import Mesh
from jax.sharding import PartitionSpec as P


PANEL = 512
X, Z, Y, C = 4, 8, 4, 2
STATE, ARCS = 6, 8
S = STATE * ARCS
PACK = S + 8
LIMIT = 12 * 2**20
HI = lax.Precision.HIGHEST
VMEM = pl.BlockSpec(memory_space=pltpu.VMEM)
SMEM = pl.BlockSpec(memory_space=pltpu.SMEM)


def call(kernel, out, n, cost, smem=()):
    flops, size = cost
    return pl.pallas_call(
        kernel,
        out_shape=out,
        in_specs=[SMEM if i in smem else VMEM for i in range(n)],
        out_specs=VMEM if not isinstance(out, (tuple, list)) else [VMEM] * len(out),
        compiler_params=pltpu.CompilerParams(vmem_limit_bytes=LIMIT),
        cost_estimate=pl.CostEstimate(flops=flops, bytes_accessed=size, transcendentals=0),
    )


def dot(a, b, ca=1, cb=0):
    return lax.dot_general(a, b, (((ca,), (cb,)), ((), ())), precision=HI, preferred_element_type=jnp.float32)


def coefficients(tile):
    spread = lambda k: jnp.broadcast_to(tile[:, k : k + 1], (ARCS, 128))
    return [[spread(c * STATE + d) for d in range(STATE)] for c in range(STATE)]


def moved(coefficient, parts):
    out = []
    for row in coefficient:
        total = row[0] * parts[0]
        for d in range(1, STATE):
            total = total + row[d] * parts[d]
        out.append(total)
    return out


def split(value):
    return [value[c * ARCS : (c + 1) * ARCS] for c in range(STATE)]


def opened(tile):
    return [tile] + [pltpu.roll(tile, 128 - c * STATE, 1) for c in range(1, STATE)]


def closed(parts):
    lane = lax.broadcasted_iota(jnp.int32, (ARCS, 128), 1)
    parts = [jnp.where(lane < STATE, part, 0.0) for part in parts]
    out = parts[0]
    for c in range(1, STATE):
        out = out + pltpu.roll(parts[c], c * STATE, 1)
    return out


def offsets_kernel(d_ref, f_ref, o_ref):
    forced = lambda j, z: split(f_ref[j, :, z * 128 : (z + 1) * 128].astype(jnp.float32))
    whole = opened(d_ref[0])
    for j in range(1, d_ref.shape[0]):
        coefficient = coefficients(d_ref[j])
        for z in range(Z):
            parts = forced(0, z) if j == 1 else split(o_ref[z, :S, :])
            parts = moved(coefficient, parts)
            o_ref[z, :S, :] = jnp.concatenate([u + v for u, v in zip(parts, forced(j, z))], 0)
        whole = moved(coefficient, whole)
    whole = closed(whole)
    for z in range(Z):
        o_ref[z, S:, :] = whole


def totals_kernel(r_ref, o_ref):
    total = split(r_ref[0, :S, :])
    whole = opened(r_ref[0, S:, :])
    for z in range(1, Z):
        coefficient = coefficients(r_ref[z, S:, :])
        total = [u + v for u, v in zip(moved(coefficient, total), split(r_ref[z, :S, :]))]
        whole = moved(coefficient, whole)
    o_ref[:S, :] = jnp.concatenate(total, 0)
    o_ref[S:, :] = closed(whole)


def incoming_kernel(at_ref, t1, t2, t3, r_ref, i_ref, o_ref):
    x = at_ref[0]
    carry = split(i_ref[:, pl.ds(pl.multiple_of(at_ref[1] * 128, 128), 128)])
    for s, ref in ((3, t3), (2, t2), (1, t1)):
        after = moved(coefficients(ref[S:, :]), carry)
        carry = [jnp.where(s <= x, u + v, w) for u, v, w in zip(after, split(ref[:S, :]), carry)]
    for z in range(Z):
        o_ref[z] = jnp.concatenate(carry, 0)
        if z < Z - 1:
            after = moved(coefficients(r_ref[z, S:, :]), carry)
            carry = [u + v for u, v in zip(after, split(r_ref[z, :S, :]))]


def design_kernel(n_ref, i_ref, d_ref, f_ref, p_ref, a_ref, o_ref, h_ref, c_ref):
    blocks = d_ref.shape[0]
    rows = p_ref.shape[1]
    length = rows // blocks
    lane = lax.broadcasted_iota(jnp.int32, (ARCS, rows), 1)
    arc = lax.broadcasted_iota(jnp.int32, (ARCS, rows), 0)
    chosen = arc == a_ref[...]
    weights = []
    for j in range(blocks):
        live = (lane >= j * length) & (lane < j * length + jnp.minimum(n_ref[j], length)) & chosen
        for c in range(STATE):
            weights.append(jnp.where(live, p_ref[c : c + 1, :], 0.0))
    weights = jnp.concatenate(weights, 0)
    for j in range(blocks):
        coefficient = coefficients(d_ref[j])
        for z in range(Z):
            at = slice(z * 128, (z + 1) * 128)
            before = i_ref[z] if j == 0 else c_ref[(j - 1) * S : j * S, at]
            parts = zip(moved(coefficient, split(before)), split(f_ref[j, :, at].astype(jnp.float32)))
            c_ref[j * S : (j + 1) * S, at] = jnp.concatenate([u + v for u, v in parts], 0)
    out = dot(weights, c_ref[...], 0, 0)
    o_ref[...] = out
    h_ref[...] = out[:, :PANEL]


def first_factor_kernel(at_ref, g_ref, m_ref, x_ref, o_ref, z_ref):
    n = z_ref.shape[0]
    half = n // C
    for c in range(C):
        source = m_ref if c else g_ref
        row = pl.multiple_of(lax.rem(at_ref[3] + c, C) * half, half)
        for u in range(Y):
            column = pl.multiple_of(lax.rem(at_ref[2] + Y - u, Y) * 128, 128)
            z_ref[pl.ds(row, half), pl.ds(column, 128)] = source[u]
    factor_block(0, x_ref, z_ref, 0, o_ref)


def second_factor_kernel(z_ref, x_ref, o_ref):
    factor_block(1, x_ref, z_ref, 128, o_ref)


def third_factor_kernel(z_ref, x_ref, o_ref):
    factor_block(2, x_ref, z_ref, 256, o_ref)


def last_factor_kernel(z_ref, x_ref):
    factor_block(3, x_ref, z_ref, 384, None)


def factor_block(k, x_ref, z_ref, top, o_ref):
    lo, hi = k * 128, k * 128 + 128
    sub = lax.broadcasted_iota(jnp.int32, (8, 128), 0)
    lane = lax.broadcasted_iota(jnp.int32, (8, 128), 1)
    i128 = lax.broadcasted_iota(jnp.int32, (128, 128), 0)
    j128 = lax.broadcasted_iota(jnp.int32, (128, 128), 1)
    wide = lambda v: jnp.broadcast_to(v, (1, 128))
    tile = lambda v: jnp.broadcast_to(v, (8, 128))
    here = slice(lo - top, hi - top)
    block = z_ref[here, lo:hi]
    part = [block[8 * g : 8 * g + 8] for g in range(16)]
    for q in range(0, 128, 2):
        gq, sq = q // 8, q % 8
        first, second = part[gq][sq : sq + 1, :], part[gq][sq + 1 : sq + 2, :]
        a, b, c = wide(first[:, q : q + 1]), wide(second[:, q : q + 1]), wide(second[:, q + 1 : q + 2])
        inverse = 1.0 / (a * c - b * b)
        l1 = lane[:1]
        one = jnp.where(l1 == q, c, jnp.where(l1 == q + 1, -b, c * first - b * second)) * inverse
        two = jnp.where(l1 == q, -b, jnp.where(l1 == q + 1, a, a * second - b * first)) * inverse
        one, two = tile(one), tile(two)
        pair = (lane == q) | (lane == q + 1)
        for g in range(gq, 16):
            if g == gq and sq == 6:
                continue
            left, right = tile(part[g][:, q : q + 1]), tile(part[g][:, q + 1 : q + 2])
            if g == gq:
                below = sub > sq + 1
                left, right = jnp.where(below, left, 0.0), jnp.where(below, right, 0.0)
                kept = jnp.where(pair & below, 0.0, part[g])
            else:
                kept = jnp.where(pair, 0.0, part[g])
            part[g] = (kept - left * one) - right * two
    done = jnp.concatenate(part, 0)
    odd = lax.rem(i128, 2) == 1
    diag = jnp.sum(jnp.where(i128 == j128, done, 0.0), axis=1, keepdims=True)
    beside = jnp.sum(jnp.where((j128 == i128 - 1) & odd, done, 0.0), axis=1, keepdims=True)
    unit = jnp.where(i128 == j128, 1.0, jnp.where(j128 < i128 - jnp.where(odd, 1, 0), done, 0.0))
    above = pltpu.roll(unit, 1, 0)
    ratio = jnp.where(odd[:, :1], beside / pltpu.roll(diag, 1, 0), 0.0)
    unit = unit - ratio * above
    pivots = diag - ratio * beside
    scale = lax.rsqrt(pivots)
    scale = scale * (1.5 - 0.5 * pivots * scale * scale)
    own = unit * scale
    x_ref[:, lo:hi] = own
    if lo:
        left = dot(own, z_ref[here, :lo])
        x_ref[:, :lo] = left
    if hi < PANEL:
        down = dot(z_ref[hi - top :, lo:hi], own, 1, 1)
        if lo:
            o_ref[:, :lo] = z_ref[hi - top :, :lo] - dot(down, left)
        o_ref[:, lo:hi] = -dot(down, own)
        o_ref[:, hi:] = z_ref[hi - top :, hi:] - dot(down, dot(own, z_ref[here, hi:]))


def factor_inverse(at, gram, mate):
    n = PANEL
    shape = lambda r, c: jax.ShapeDtypeStruct((r, c), jnp.float32)
    step = lambda kernel, out, ins, scratch, k: pl.pallas_call(
        kernel,
        out_shape=out,
        in_specs=ins,
        out_specs=[VMEM] * len(out),
        scratch_shapes=scratch,
        compiler_params=pltpu.CompilerParams(vmem_limit_bytes=LIMIT),
        cost_estimate=pl.CostEstimate(flops=k * 10**10, bytes_accessed=n * n * 4, transcendentals=0),
    )
    square = [pltpu.VMEM((n, n), jnp.float32)]
    l0, z = step(first_factor_kernel, [shape(128, 128), shape(384, n)], [SMEM, VMEM, VMEM], square, 1)(at, gram, mate)
    l1, z = step(second_factor_kernel, [shape(128, 256), shape(256, n)], [VMEM], [], 1)(z)
    l2, z = step(third_factor_kernel, [shape(128, 384), shape(128, n)], [VMEM], [], 1)(z)
    (l3,) = step(last_factor_kernel, [shape(128, n)], [VMEM], [], 1)(z)
    return l0, l1, l2, l3


def assembled(at_ref, refs, g_ref):
    step = PANEL // X
    for s, ref in zip((0, 2, 1, 3), refs):
        row = pl.multiple_of(lax.rem(at_ref[0] + X - s, X) * step, step)
        g_ref[pl.ds(row, step), :] = ref[...]


def first_final_kernel(mid, at_ref, l0, l1, l2, l3, p_ref, m_ref, b0, b1, b2, b3, o_ref, r_ref, q_ref, g_ref):
    root = math.sqrt(X * Z * p_ref.shape[0])
    p = at_ref[2] * C + at_ref[3]
    q_ref[...] = jnp.concatenate([dot(p_ref[:, : l.shape[1]], l[...], 1, 1) for l in (l0, l1, l2, l3)], 1)
    assembled(at_ref, (b0, b1, b2, b3), g_ref)

    def columns(t, _):
        at = pl.ds(pl.multiple_of(t * 256, 256), 256)
        rows = jnp.concatenate([dot(l[...], g_ref[: l.shape[1], at]) for l in (l0, l1, l2, l3)], 0)
        r_ref[:, at] = rows * (1.0 / root)
        updated = m_ref[:, at] - dot(q_ref[...], rows)
        head = q_ref[:, pl.ds(pl.multiple_of(lax.rem(t, PANEL // 256) * 256, 256), 256)] * root
        o_ref[:, at] = jnp.where((p == 0) & (t < PANEL // 256), head, updated)
        return 0

    lax.fori_loop(0, mid // 256, columns, 0)


def second_final_kernel(at_ref, l0, l1, l2, l3, q_ref, m_ref, b0, b1, b2, b3, o_in, r_in, o_ref, r_ref, g_ref):
    root = math.sqrt(X * Z * q_ref.shape[0])
    assembled(at_ref, (b0, b1, b2, b3), g_ref)

    def columns(t, _):
        at = pl.ds(pl.multiple_of(t * 256, 256), 256)
        rows = jnp.concatenate([dot(l[...], g_ref[: l.shape[1], at]) for l in (l0, l1, l2, l3)], 0)
        r_ref[:, at] = rows * (1.0 / root)
        o_ref[:, at] = m_ref[:, at] - dot(q_ref[...], rows)
        return 0

    lax.fori_loop(0, m_ref.shape[1] // 256, columns, 0)


def exchanged(blocks, axis):
    return lax.all_to_all(blocks, axis, 0, 0, tiled=False)


def everywhere(block, axis, size):
    return exchanged(jnp.broadcast_to(block[None], (size,) + block.shape), axis)


def shift(block, axis, size, by):
    return lax.ppermute(block, axis, [(i, (i + by) % size) for i in range(size)])


def local(initial_carry, forcing, transition, partials, arc_of_row, counts):
    f32 = jnp.float32
    x, z = lax.axis_index("x"), lax.axis_index("z")
    p = lax.axis_index(("y", "core"))
    width = initial_carry.shape[1]
    rows = partials.shape[1]
    blocks = transition.shape[0]
    core, y = lax.axis_index("core"), lax.axis_index("y")
    at = jnp.stack([x, z, y, core])
    maps = transition.transpose(0, 3, 1, 2).reshape(blocks, ARCS, STATE * STATE)
    maps = jnp.pad(maps, ((0, 0), (0, 0), (0, 128 - STATE * STATE)))

    packed = call(offsets_kernel, jax.ShapeDtypeStruct((Z, PACK, 128), f32), 2, (10**7, 10**6))(maps, forcing)
    received = exchanged(packed, "z")
    total = call(totals_kernel, jax.ShapeDtypeStruct((PACK, 128), f32), 1, (10**6, 10**5))(received)
    totals = [shift(total, "x", X, k) for k in range(1, X)]
    incoming = call(incoming_kernel, jax.ShapeDtypeStruct((Z, S, 128), f32), 6, (10**6, 10**5), (0,))(
        at, *totals, received, initial_carry
    )
    incoming = exchanged(incoming, "z")
    matrix, panel = pl.pallas_call(
        design_kernel,
        out_shape=[jax.ShapeDtypeStruct((rows, width), f32), jax.ShapeDtypeStruct((rows, PANEL), f32)],
        in_specs=[SMEM] + [VMEM] * 5,
        out_specs=[VMEM, VMEM],
        scratch_shapes=[pltpu.VMEM((blocks * S, width), f32)],
        compiler_params=pltpu.CompilerParams(vmem_limit_bytes=LIMIT),
        cost_estimate=pl.CostEstimate(flops=10**8, bytes_accessed=10**6, transcendentals=0),
    )(counts, incoming, maps, forcing, partials, arc_of_row[None, :])

    both = ("y", "core")
    right, far, left = [lax.ppermute(panel, both, [(0, k)]) for k in (2, 4, 6)]
    panel = jnp.where(p == 2, right, jnp.where(p == 4, far, jnp.where(p == 6, left, panel)))
    other = lax.ppermute(panel, both, [(0, 1), (2, 3), (4, 5), (6, 7)])
    panel = jnp.where(lax.axis_index("core") == 1, other, panel)

    half, quarter, step = PANEL // C, PANEL // Y, PANEL // X
    tile, mid = step // Z, 3 * width // 4
    gram = dot(
        lax.dynamic_slice(panel, (0, core * half), (rows, half)),
        lax.dynamic_slice(panel, (0, y * quarter), (rows, quarter)),
        0, 0,
    )
    gram, panel = lax.optimization_barrier((gram, panel))
    gram = exchanged(gram.reshape(X * Z, half // X // Z, quarter), ("x", "z"))
    gram = gram.sum(0)
    turned = lax.dynamic_slice(jnp.concatenate([panel, panel], 1), (0, x * step), (rows, PANEL))
    parts = [dot(turned[:, k * step : (k + 1) * step], matrix, 0, 0) for k in range(X)]
    sent = [shift(parts[k], "x", X, k) for k in (2, 1, 3)]
    gram = everywhere(gram, ("x", "z"), X * Z).reshape(half, quarter)
    gram, sent = lax.optimization_barrier((gram, sent))
    gram = [gram] + [shift(gram, "y", Y, k) for k in (1, 2, 3)]
    gram = jnp.stack(gram, 0)
    mate = lax.ppermute(gram, "core", [(0, 1), (1, 0)])

    products = parts[0] + sent[0] + sent[1] + sent[2]
    products = exchanged(products.reshape(Z, tile, width), "z")
    products = products.sum(0)
    products = everywhere(products, "z", Z)
    products = products.reshape(step, width)
    a = [products[:, :mid]]
    a += [shift(a[0], "x", X, k) for k in (2, 1, 3)]
    b = [products[:, mid:]]
    b += [shift(b[0], "x", X, k) for k in (2, 1, 3)]

    inverse = factor_inverse(at, gram, mate)
    half = jax.ShapeDtypeStruct((rows, width), f32), jax.ShapeDtypeStruct((PANEL, width), f32)
    packed, r_rows, basis = pl.pallas_call(
        functools.partial(first_final_kernel, mid),
        grid=(1,),
        out_shape=[*half, jax.ShapeDtypeStruct((rows, PANEL), f32)],
        in_specs=[SMEM] + [VMEM] * 10,
        out_specs=[pl.BlockSpec((rows, mid), lambda i: (0, 0)), pl.BlockSpec((PANEL, mid), lambda i: (0, 0)), VMEM],
        scratch_shapes=[pltpu.VMEM((PANEL, mid), f32)],
        compiler_params=pltpu.CompilerParams(vmem_limit_bytes=LIMIT),
        cost_estimate=pl.CostEstimate(flops=2 * 10**9, bytes_accessed=3 * 10**6, transcendentals=0),
    )(at, *inverse, panel, matrix[:, :mid], *a)
    return pl.pallas_call(
        second_final_kernel,
        grid=(1,),
        out_shape=half,
        in_specs=[SMEM] + [VMEM] * 10 + [pl.BlockSpec(memory_space=pl.ANY)] * 2,
        out_specs=[pl.BlockSpec((rows, width - mid), lambda i: (0, 3)), pl.BlockSpec((PANEL, width - mid), lambda i: (0, 3))],
        scratch_shapes=[pltpu.VMEM((PANEL, width - mid), f32)],
        input_output_aliases={11: 0, 12: 1},
        compiler_params=pltpu.CompilerParams(vmem_limit_bytes=LIMIT),
        cost_estimate=pl.CostEstimate(flops=2 * 10**9, bytes_accessed=3 * 10**6, transcendentals=0),
    )(at, *inverse, basis, matrix[:, mid:], *b, packed, r_rows)


def solution(mesh):
    mesh = Mesh(mesh.devices.reshape(X, Z, Y, C), ("x", "z", "y", "core"))
    e, q = ("x", "z"), ("y", "core")
    return jax.shard_map(
        local,
        mesh=mesh,
        in_specs=(P(None, q), P(e, None, q), P(e, None, None, None), P(None, e), P(e), P(e)),
        out_specs=(P(e, q), P(None, q)),
        check_vma=False,
    )
```

```python
import functools
import math

import jax
import jax.numpy as jnp
from jax import lax
from jax.experimental import pallas as pl
from jax.experimental.pallas import tpu as pltpu
from jax.sharding import Mesh
from jax.sharding import PartitionSpec as P


PANEL = 512
X, Z, Y, C = 4, 8, 4, 2
STATE, ARCS = 6, 8
S = STATE * ARCS
PACK = S + 8
LIMIT = 12 * 2**20
HI = lax.Precision.HIGHEST
VMEM = pl.BlockSpec(memory_space=pltpu.VMEM)
SMEM = pl.BlockSpec(memory_space=pltpu.SMEM)


def call(kernel, out, n, cost, smem=()):
    flops, size = cost
    return pl.pallas_call(
        kernel,
        out_shape=out,
        in_specs=[SMEM if i in smem else VMEM for i in range(n)],
        out_specs=VMEM if not isinstance(out, (tuple, list)) else [VMEM] * len(out),
        compiler_params=pltpu.CompilerParams(vmem_limit_bytes=LIMIT),
        cost_estimate=pl.CostEstimate(flops=flops, bytes_accessed=size, transcendentals=0),
    )


def dot(a, b, ca=1, cb=0):
    return lax.dot_general(a, b, (((ca,), (cb,)), ((), ())), precision=HI, preferred_element_type=jnp.float32)


def coefficients(tile):
    spread = lambda k: jnp.broadcast_to(tile[:, k : k + 1], (ARCS, 128))
    return [[spread(c * STATE + d) for d in range(STATE)] for c in range(STATE)]


def moved(coefficient, parts):
    out = []
    for row in coefficient:
        total = row[0] * parts[0]
        for d in range(1, STATE):
            total = total + row[d] * parts[d]
        out.append(total)
    return out


def split(value):
    return [value[c * ARCS : (c + 1) * ARCS] for c in range(STATE)]


def opened(tile):
    return [tile] + [pltpu.roll(tile, 128 - c * STATE, 1) for c in range(1, STATE)]


def closed(parts):
    lane = lax.broadcasted_iota(jnp.int32, (ARCS, 128), 1)
    parts = [jnp.where(lane < STATE, part, 0.0) for part in parts]
    out = parts[0]
    for c in range(1, STATE):
        out = out + pltpu.roll(parts[c], c * STATE, 1)
    return out


def offsets_kernel(d_ref, f_ref, o_ref):
    forced = lambda j, z: split(f_ref[j, :, z * 128 : (z + 1) * 128].astype(jnp.float32))
    whole = opened(d_ref[0])
    for j in range(1, d_ref.shape[0]):
        coefficient = coefficients(d_ref[j])
        for z in range(Z):
            parts = forced(0, z) if j == 1 else split(o_ref[z, :S, :])
            parts = moved(coefficient, parts)
            o_ref[z, :S, :] = jnp.concatenate([u + v for u, v in zip(parts, forced(j, z))], 0)
        whole = moved(coefficient, whole)
    whole = closed(whole)
    for z in range(Z):
        o_ref[z, S:, :] = whole


def totals_kernel(r_ref, o_ref):
    total = split(r_ref[0, :S, :])
    whole = opened(r_ref[0, S:, :])
    for z in range(1, Z):
        coefficient = coefficients(r_ref[z, S:, :])
        total = [u + v for u, v in zip(moved(coefficient, total), split(r_ref[z, :S, :]))]
        whole = moved(coefficient, whole)
    o_ref[:S, :] = jnp.concatenate(total, 0)
    o_ref[S:, :] = closed(whole)


def incoming_kernel(at_ref, t1, t2, t3, r_ref, i_ref, o_ref):
    x = at_ref[0]
    carry = split(i_ref[:, pl.ds(pl.multiple_of(at_ref[1] * 128, 128), 128)])
    for s, ref in ((3, t3), (2, t2), (1, t1)):
        after = moved(coefficients(ref[S:, :]), carry)
        carry = [jnp.where(s <= x, u + v, w) for u, v, w in zip(after, split(ref[:S, :]), carry)]
    for z in range(Z):
        o_ref[z] = jnp.concatenate(carry, 0)
        if z < Z - 1:
            after = moved(coefficients(r_ref[z, S:, :]), carry)
            carry = [u + v for u, v in zip(after, split(r_ref[z, :S, :]))]


def design_kernel(n_ref, i_ref, d_ref, f_ref, p_ref, a_ref, o_ref, h_ref, c_ref):
    blocks = d_ref.shape[0]
    rows = p_ref.shape[1]
    length = rows // blocks
    lane = lax.broadcasted_iota(jnp.int32, (ARCS, rows), 1)
    arc = lax.broadcasted_iota(jnp.int32, (ARCS, rows), 0)
    chosen = arc == a_ref[...]
    weights = []
    for j in range(blocks):
        live = (lane >= j * length) & (lane < j * length + jnp.minimum(n_ref[j], length)) & chosen
        for c in range(STATE):
            weights.append(jnp.where(live, p_ref[c : c + 1, :], 0.0))
    weights = jnp.concatenate(weights, 0)
    for j in range(blocks):
        coefficient = coefficients(d_ref[j])
        for z in range(Z):
            at = slice(z * 128, (z + 1) * 128)
            before = i_ref[z] if j == 0 else c_ref[(j - 1) * S : j * S, at]
            parts = zip(moved(coefficient, split(before)), split(f_ref[j, :, at].astype(jnp.float32)))
            c_ref[j * S : (j + 1) * S, at] = jnp.concatenate([u + v for u, v in parts], 0)
    out = dot(weights, c_ref[...], 0, 0)
    o_ref[...] = out
    h_ref[...] = out[:, :PANEL]


def first_factor_kernel(at_ref, g_ref, m_ref, x_ref, o_ref, z_ref):
    n = z_ref.shape[0]
    half = n // C
    for c in range(C):
        source = m_ref if c else g_ref
        row = pl.multiple_of(lax.rem(at_ref[3] + c, C) * half, half)
        for u in range(Y):
            column = pl.multiple_of(lax.rem(at_ref[2] + Y - u, Y) * 128, 128)
            z_ref[pl.ds(row, half), pl.ds(column, 128)] = source[u]
    factor_block(0, x_ref, z_ref, 0, o_ref)


def second_factor_kernel(z_ref, x_ref, o_ref):
    factor_block(1, x_ref, z_ref, 128, o_ref)


def third_factor_kernel(z_ref, x_ref, o_ref):
    factor_block(2, x_ref, z_ref, 256, o_ref)


def last_factor_kernel(z_ref, x_ref):
    factor_block(3, x_ref, z_ref, 384, None)


def factor_block(k, x_ref, z_ref, top, o_ref):
    lo, hi = k * 128, k * 128 + 128
    sub = lax.broadcasted_iota(jnp.int32, (8, 128), 0)
    lane = lax.broadcasted_iota(jnp.int32, (8, 128), 1)
    i128 = lax.broadcasted_iota(jnp.int32, (128, 128), 0)
    j128 = lax.broadcasted_iota(jnp.int32, (128, 128), 1)
    wide = lambda v: jnp.broadcast_to(v, (1, 128))
    tile = lambda v: jnp.broadcast_to(v, (8, 128))
    here = slice(lo - top, hi - top)
    block = z_ref[here, lo:hi]
    part = [block[8 * g : 8 * g + 8] for g in range(16)]
    for q in range(0, 128, 2):
        gq, sq = q // 8, q % 8
        first, second = part[gq][sq : sq + 1, :], part[gq][sq + 1 : sq + 2, :]
        a, b, c = wide(first[:, q : q + 1]), wide(second[:, q : q + 1]), wide(second[:, q + 1 : q + 2])
        inverse = 1.0 / (a * c - b * b)
        l1 = lane[:1]
        one = jnp.where(l1 == q, c, jnp.where(l1 == q + 1, -b, c * first - b * second)) * inverse
        two = jnp.where(l1 == q, -b, jnp.where(l1 == q + 1, a, a * second - b * first)) * inverse
        one, two = tile(one), tile(two)
        pair = (lane == q) | (lane == q + 1)
        for g in range(gq, 16):
            if g == gq and sq == 6:
                continue
            left, right = tile(part[g][:, q : q + 1]), tile(part[g][:, q + 1 : q + 2])
            if g == gq:
                below = sub > sq + 1
                left, right = jnp.where(below, left, 0.0), jnp.where(below, right, 0.0)
                kept = jnp.where(pair & below, 0.0, part[g])
            else:
                kept = jnp.where(pair, 0.0, part[g])
            part[g] = (kept - left * one) - right * two
    done = jnp.concatenate(part, 0)
    odd = lax.rem(i128, 2) == 1
    diag = jnp.sum(jnp.where(i128 == j128, done, 0.0), axis=1, keepdims=True)
    beside = jnp.sum(jnp.where((j128 == i128 - 1) & odd, done, 0.0), axis=1, keepdims=True)
    unit = jnp.where(i128 == j128, 1.0, jnp.where(j128 < i128 - jnp.where(odd, 1, 0), done, 0.0))
    above = pltpu.roll(unit, 1, 0)
    ratio = jnp.where(odd[:, :1], beside / pltpu.roll(diag, 1, 0), 0.0)
    unit = unit - ratio * above
    pivots = diag - ratio * beside
    scale = lax.rsqrt(pivots)
    scale = scale * (1.5 - 0.5 * pivots * scale * scale)
    own = unit * scale
    x_ref[:, lo:hi] = own
    if lo:
        left = dot(own, z_ref[here, :lo])
        x_ref[:, :lo] = left
    if hi < PANEL:
        down = dot(z_ref[hi - top :, lo:hi], own, 1, 1)
        if lo:
            o_ref[:, :lo] = z_ref[hi - top :, :lo] - dot(down, left)
        o_ref[:, lo:hi] = -dot(down, own)
        o_ref[:, hi:] = z_ref[hi - top :, hi:] - dot(down, dot(own, z_ref[here, hi:]))


def factor_inverse(at, gram, mate):
    n = PANEL
    shape = lambda r, c: jax.ShapeDtypeStruct((r, c), jnp.float32)
    step = lambda kernel, out, ins, scratch, k: pl.pallas_call(
        kernel,
        out_shape=out,
        in_specs=ins,
        out_specs=[VMEM] * len(out),
        scratch_shapes=scratch,
        compiler_params=pltpu.CompilerParams(vmem_limit_bytes=LIMIT),
        cost_estimate=pl.CostEstimate(flops=k * 10**10, bytes_accessed=n * n * 4, transcendentals=0),
    )
    square = [pltpu.VMEM((n, n), jnp.float32)]
    l0, z = step(first_factor_kernel, [shape(128, 128), shape(384, n)], [SMEM, VMEM, VMEM], square, 1)(at, gram, mate)
    l1, z = step(second_factor_kernel, [shape(128, 256), shape(256, n)], [VMEM], [], 1)(z)
    l2, z = step(third_factor_kernel, [shape(128, 384), shape(128, n)], [VMEM], [], 1)(z)
    (l3,) = step(last_factor_kernel, [shape(128, n)], [VMEM], [], 1)(z)
    return l0, l1, l2, l3


def assembled(at_ref, refs, g_ref):
    step = PANEL // X
    for s, ref in zip((0, 2, 1, 3), refs):
        row = pl.multiple_of(lax.rem(at_ref[0] + X - s, X) * step, step)
        g_ref[pl.ds(row, step), :] = ref[...]


def first_final_kernel(mid, at_ref, l0, l1, l2, l3, p_ref, m_ref, b0, b1, b2, b3, o_ref, r_ref, q_ref, g_ref):
    root = math.sqrt(X * Z * p_ref.shape[0])
    p = at_ref[2] * C + at_ref[3]
    q_ref[...] = jnp.concatenate([dot(p_ref[:, : l.shape[1]], l[...], 1, 1) for l in (l0, l1, l2, l3)], 1)
    assembled(at_ref, (b0, b1, b2, b3), g_ref)

    def columns(t, _):
        at = pl.ds(pl.multiple_of(t * 256, 256), 256)
        rows = jnp.concatenate([dot(l[...], g_ref[: l.shape[1], at]) for l in (l0, l1, l2, l3)], 0)
        r_ref[:, at] = rows * (1.0 / root)
        updated = m_ref[:, at] - dot(q_ref[...], rows)
        o_ref[:, at] = jnp.where(p == 0, q_ref[:, at] * root, updated)
        return 0

    lax.fori_loop(0, mid // 256, columns, 0)


def second_final_kernel(at_ref, l0, l1, l2, l3, q_ref, m_ref, b0, b1, b2, b3, o_in, r_in, o_ref, r_ref, g_ref):
    root = math.sqrt(X * Z * q_ref.shape[0])
    assembled(at_ref, (b0, b1, b2, b3), g_ref)

    def columns(t, _):
        at = pl.ds(pl.multiple_of(t * 256, 256), 256)
        rows = jnp.concatenate([dot(l[...], g_ref[: l.shape[1], at]) for l in (l0, l1, l2, l3)], 0)
        r_ref[:, at] = rows * (1.0 / root)
        o_ref[:, at] = m_ref[:, at] - dot(q_ref[...], rows)
        return 0

    lax.fori_loop(0, m_ref.shape[1] // 256, columns, 0)


def sum_tile_kernel(a_ref, o_ref):
    total = a_ref[0]
    for z in range(1, Z):
        total = total + a_ref[z]
    for z in range(Z):
        o_ref[z] = total


def exchanged(blocks, axis):
    return lax.all_to_all(blocks, axis, 0, 0, tiled=False)


def everywhere(block, axis, size):
    return exchanged(jnp.broadcast_to(block[None], (size,) + block.shape), axis)


def shift(block, axis, size, by):
    return lax.ppermute(block, axis, [(i, (i + by) % size) for i in range(size)])


def local(initial_carry, forcing, transition, partials, arc_of_row, counts):
    f32 = jnp.float32
    x, z = lax.axis_index("x"), lax.axis_index("z")
    p = lax.axis_index(("y", "core"))
    width = initial_carry.shape[1]
    rows = partials.shape[1]
    blocks = transition.shape[0]
    core, y = lax.axis_index("core"), lax.axis_index("y")
    at = jnp.stack([x, z, y, core])
    maps = transition.transpose(0, 3, 1, 2).reshape(blocks, ARCS, STATE * STATE)
    maps = jnp.pad(maps, ((0, 0), (0, 0), (0, 128 - STATE * STATE)))

    packed = call(offsets_kernel, jax.ShapeDtypeStruct((Z, PACK, 128), f32), 2, (10**7, 10**6))(maps, forcing)
    received = exchanged(packed, "z")
    total = call(totals_kernel, jax.ShapeDtypeStruct((PACK, 128), f32), 1, (10**6, 10**5))(received)
    totals = [shift(total, "x", X, k) for k in range(1, X)]
    incoming = call(incoming_kernel, jax.ShapeDtypeStruct((Z, S, 128), f32), 6, (10**6, 10**5), (0,))(
        at, *totals, received, initial_carry
    )
    incoming = exchanged(incoming, "z")
    matrix, panel = pl.pallas_call(
        design_kernel,
        out_shape=[jax.ShapeDtypeStruct((rows, width), f32), jax.ShapeDtypeStruct((rows, PANEL), f32)],
        in_specs=[SMEM] + [VMEM] * 5,
        out_specs=[VMEM, VMEM],
        scratch_shapes=[pltpu.VMEM((blocks * S, width), f32)],
        compiler_params=pltpu.CompilerParams(vmem_limit_bytes=LIMIT),
        cost_estimate=pl.CostEstimate(flops=10**8, bytes_accessed=10**6, transcendentals=0),
    )(counts, incoming, maps, forcing, partials, arc_of_row[None, :])

    both = ("y", "core")
    right, far, left = [lax.ppermute(panel, both, [(0, k)]) for k in (2, 4, 6)]
    panel = jnp.where(p == 2, right, jnp.where(p == 4, far, jnp.where(p == 6, left, panel)))
    other = lax.ppermute(panel, both, [(0, 1), (2, 3), (4, 5), (6, 7)])
    panel = jnp.where(lax.axis_index("core") == 1, other, panel)

    half, quarter, step = PANEL // C, PANEL // Y, PANEL // X
    tile, mid = step // Z, PANEL
    gram = dot(
        lax.dynamic_slice(panel, (0, core * half), (rows, half)),
        lax.dynamic_slice(panel, (0, y * quarter), (rows, quarter)),
        0, 0,
    )
    gram, panel = lax.optimization_barrier((gram, panel))
    gram = exchanged(gram.reshape(X * Z, half // X // Z, quarter), ("x", "z"))
    gram = gram.sum(0)
    turned = lax.dynamic_slice(jnp.concatenate([panel, panel], 1), (0, x * step), (rows, PANEL))
    parts = [dot(turned[:, k * step : (k + 1) * step], matrix, 0, 0) for k in range(X)]
    sent = [shift(parts[k], "x", X, k) for k in (2, 1, 3)]
    gram = everywhere(gram, ("x", "z"), X * Z).reshape(half, quarter)
    gram, sent = lax.optimization_barrier((gram, sent))
    gram = [gram] + [shift(gram, "y", Y, k) for k in (1, 2, 3)]
    gram = jnp.stack(gram, 0)
    mate = lax.ppermute(gram, "core", [(0, 1), (1, 0)])

    products = parts[0] + sent[0] + sent[1] + sent[2]
    products = exchanged(products.reshape(Z, tile, width), "z")
    products = call(sum_tile_kernel, jax.ShapeDtypeStruct((Z, tile, width), f32), 1, (10**6, 10**6))(products)
    products = exchanged(products, "z")
    products = products.reshape(step, width)
    a = [products[:, :mid]]
    a += [shift(a[0], "x", X, k) for k in (2, 1, 3)]
    b = [products[:, mid:]]
    b += [shift(b[0], "x", X, k) for k in (2, 1, 3)]

    inverse = factor_inverse(at, gram, mate)
    half = jax.ShapeDtypeStruct((rows, width), f32), jax.ShapeDtypeStruct((PANEL, width), f32)
    packed, r_rows, basis = pl.pallas_call(
        functools.partial(first_final_kernel, mid),
        grid=(1,),
        out_shape=[*half, jax.ShapeDtypeStruct((rows, PANEL), f32)],
        in_specs=[SMEM] + [VMEM] * 10,
        out_specs=[pl.BlockSpec((rows, mid), lambda i: (0, 0)), pl.BlockSpec((PANEL, mid), lambda i: (0, 0)), VMEM],
        scratch_shapes=[pltpu.VMEM((PANEL, mid), f32)],
        compiler_params=pltpu.CompilerParams(vmem_limit_bytes=LIMIT),
        cost_estimate=pl.CostEstimate(flops=2 * 10**9, bytes_accessed=3 * 10**6, transcendentals=0),
    )(at, *inverse, panel, matrix[:, :mid], *a)
    return pl.pallas_call(
        second_final_kernel,
        grid=(1,),
        out_shape=half,
        in_specs=[SMEM] + [VMEM] * 10 + [pl.BlockSpec(memory_space=pl.ANY)] * 2,
        out_specs=[pl.BlockSpec((rows, width - mid), lambda i: (0, 1)), pl.BlockSpec((PANEL, width - mid), lambda i: (0, 1))],
        scratch_shapes=[pltpu.VMEM((PANEL, width - mid), f32)],
        input_output_aliases={11: 0, 12: 1},
        compiler_params=pltpu.CompilerParams(vmem_limit_bytes=LIMIT),
        cost_estimate=pl.CostEstimate(flops=2 * 10**9, bytes_accessed=3 * 10**6, transcendentals=0),
    )(at, *inverse, basis, matrix[:, mid:], *b, packed, r_rows)


def solution(mesh):
    mesh = Mesh(mesh.devices.reshape(X, Z, Y, C), ("x", "z", "y", "core"))
    e, q = ("x", "z"), ("y", "core")
    return jax.shard_map(
        local,
        mesh=mesh,
        in_specs=(P(None, q), P(e, None, q), P(e, None, None, None), P(None, e), P(e), P(e)),
        out_specs=(P(e, q), P(None, q)),
        check_vma=False,
    )
```
